256 devices in a mesh: tm: 32 (over y, z_lo, core), space: 8 (over z_hi, x).
Axes of the slice: x: 4, y: 4, z: 8 (z_hi: 2, z_lo: 4; z = z_hi * 4 + z_lo), core: 2. Of those that a mesh axis runs over, the one named last changes fastest.
Arguments:
- c_points: float32 [64, 3, 256, 512], P('tm', None, 'space'), may hold values from -0.45 to 1.3, as said below
Outputs:
- updated: float32 [64, 3, 256, 512], P('tm', None, 'space')
- coarse_residual: float32 [64, 3, 8, 32, 512], P(None, None, 'space', 'tm')
The draws below stay inside these ranges and needn't reach their ends.
Inputs may be any that keep to these rules, and one draw needn't show every extreme that they name: `c_points`: the first field (height) lies in 0.7 to 1.3, the other two (momenta) in -0.45 to 0.45.
All inputs are finite; a program needn't handle non-finite values.
Results may differ from the reference program's by a relative error of at most 0.000028.
Values sent between devices are 32-bit elements; how exact they have to be, the bound alone decides.
A program may use at most 64 MiB of HBM per device.

```python
import jax
import jax.numpy as jnp
from jax import lax

FACTOR = 8
STRIP_ROWS = 32
COLUMNS = 512
COARSE = 64
GRID_ROWS = 256
N_SPACE = 8


def draw_c_points(key, part):
    keys = jax.random.split(key, 3)
    shape = (COARSE, GRID_ROWS, COLUMNS)
    height = 1.0 + 0.3 * jax.random.uniform(keys[0], shape, jnp.float32, -1.0, 1.0)
    east_flow = jnp.clip(0.15 * jax.random.normal(keys[1], shape, jnp.float32), -0.45, 0.45)
    north_flow = jnp.clip(0.15 * jax.random.normal(keys[2], shape, jnp.float32), -0.45, 0.45)
    return jnp.stack([height, east_flow, north_flow], axis=1).astype(jnp.float32)


def setup_inputs(seed: int = 0) -> dict:
    key_of = jax.random.split(jax.random.key(seed), 2)
    c_points = draw_c_points(jax.random.fold_in(key_of[1], 71), 0)
    return dict(c_points=c_points)


gravity = 1.0
half_ratio = 0.1


def column_flux(state):
    height = state[..., 0, :, :]
    east_flow = state[..., 1, :, :]
    north_flow = state[..., 2, :, :]
    velocity = east_flow / height
    return jnp.stack([east_flow, east_flow * velocity + 0.5 * gravity * height * height, north_flow * velocity], axis=-3)


def row_flux(state):
    height = state[..., 0, :, :]
    east_flow = state[..., 1, :, :]
    north_flow = state[..., 2, :, :]
    velocity = north_flow / height
    return jnp.stack([north_flow, east_flow * velocity, north_flow * velocity + 0.5 * gravity * height * height], axis=-3)


def flux_step(extended):
    center = extended[..., 1:-1, :]
    upper_row = extended[..., 2:, :]
    lower_row = extended[..., :-2, :]
    right_cells = jnp.roll(center, -1, axis=-1)
    left_cells = jnp.roll(center, 1, axis=-1)
    average = 0.25 * (upper_row + lower_row + right_cells + left_cells)
    return average - half_ratio * (column_flux(right_cells) - column_flux(left_cells)) - half_ratio * (row_flux(upper_row) - row_flux(lower_row))


def propagate(state):
    for step in range(FACTOR):
        extended = jnp.concatenate([state[:, -1:, :], state, state[:, :1, :]], axis=1)
        state = flux_step(extended)
    return state


def reference(c_points):
    advanced = lax.map(propagate, c_points)
    updated = jnp.concatenate([c_points[:1], advanced[:-1]], axis=0)
    pushed = lax.map(propagate, updated)
    residual = (pushed - advanced).reshape(COARSE, 3, N_SPACE, STRIP_ROWS, COLUMNS)
    return updated, residual
```

```python
import jax
import jax.numpy as jnp
from jax import lax
from jax.experimental import pallas as pl
from jax.experimental.pallas import tpu as pltpu
from jax.sharding import PartitionSpec as P

FACTOR = 8
LANES = 128
HALO = 2 * FACTOR
SUBLANES = 8
MOMENTUM_SCALE = 0.4
SQUARE_SCALE = 0.08
MESH = pl.DeviceIdType.MESH


def inverse(height):
    return 1.0 / height


def step_rows(src, dst, square):
    count = src.shape[1]
    columns = src.shape[3]

    def parts(b):
        h, p, q = src[0, b], src[1, b], src[2, b]
        r = inverse(h)
        u = p * r
        v = q * r
        mixed = u * q
        half = (h * square) * h
        east = u * p + half
        north = v * q + half
        from_east = (h - p, p - east, q - mixed)
        from_west = (h + p, p + east, q + mixed)
        from_north = (h - q, p - mixed, q - north)
        from_south = (h + q, p + mixed, q + north)
        across = [
            pltpu.roll(e, columns - 1, axis=1) + pltpu.roll(w, 1, axis=1)
            for e, w in zip(from_east, from_west)
        ]
        return across, from_north, from_south

    def put(b, across, north, south):
        for f in range(3):
            dst[f, b] = across[f] + (north[f] + south[f])

    first = parts(0)
    second = parts(1)
    older, old = first, second
    for b in range(2, count):
        new = parts(b)
        put(b - 1, old[0], new[1], older[2])
        older, old = old, new
    put(count - 1, old[0], [pltpu.roll(x, SUBLANES - 1, axis=0) for x in first[1]], older[2])
    put(0, first[0], second[1], [pltpu.roll(x, 1, axis=0) for x in old[2]])


def kernel(c_ref, updated, coarse, ext, states, settled, behind, stage,
           local_sem, halo_send, halo_recv, shift_send, shift_recv, row_send, row_recv):
    t = lax.axis_index("tm")
    s = lax.axis_index("space")
    times = lax.axis_size("tm")
    strips = lax.axis_size("space")
    rows, columns = c_ref.shape[2], c_ref.shape[3]
    blocks = columns // LANES
    full = rows + 2 * HALO
    count = full // SUBLANES
    low = lax.rem(s + strips - 1, strips)
    high = lax.rem(s + 1, strips)
    before = lax.rem(t + times - 1, times)
    after = lax.rem(t + 1, times)

    barrier = pltpu.get_barrier_semaphore()

    @pl.loop(1, times)
    def _(d):
        pl.semaphore_signal(barrier, inc=1, device_id=(lax.rem(t + d, times), s), device_id_type=MESH)

    for neighbour in (low, high):
        pl.semaphore_signal(barrier, inc=1, device_id=(t, neighbour), device_id_type=MESH)

    lanes = [pl.ds(i * LANES, LANES) for i in range(blocks)]
    own = [
        [
            pltpu.make_async_copy(
                c_ref.at[k, :, :, lanes[i]], ext.at[k, :, i, pl.ds(HALO, rows), :], local_sem.at[k]
            )
            for i in range(blocks)
        ]
        for k in range(2)
    ]
    for k in range(2):
        for copy in own[k]:
            copy.start()
    opening = pltpu.make_async_copy(c_ref.at[0], updated.at[0], local_sem.at[2])

    @pl.when(t == 0)
    def _():
        opening.start()

    pl.semaphore_wait(barrier, times + 1)

    for k in range(2):
        for i in range(blocks):
            for target, source, place in ((high, rows - HALO, 0), (low, 0, HALO + rows)):
                pltpu.make_async_remote_copy(
                    src_ref=c_ref.at[k, :, pl.ds(source, HALO), lanes[i]],
                    dst_ref=ext.at[k, :, i, pl.ds(place, HALO), :],
                    send_sem=halo_send.at[k],
                    recv_sem=halo_recv.at[k],
                    device_id=(t, target),
                    device_id_type=MESH,
                ).start()

    def halo_bytes(k):
        part = ext.at[k, :, :, pl.ds(0, 2 * HALO), :]
        return pltpu.make_async_remote_copy(
            src_ref=part, dst_ref=part, send_sem=halo_send.at[k], recv_sem=halo_recv.at[k],
            device_id=(t, high), device_id_type=MESH,
        )

    def propagate(k, square):
        a, b = states.at[k, 0], states.at[k, 1]

        def two(_, square):
            step_rows(a, b, square)
            square = square * 0.25
            step_rows(b, a, square)
            return square * 0.25

        return lax.fori_loop(0, FACTOR // 2, two, square)

    down = [0.25 ** (2 * FACTOR), 0.25 ** (2 * FACTOR) / MOMENTUM_SCALE, 0.25 ** (2 * FACTOR) / MOMENTUM_SCALE]
    middle = [0.25 ** FACTOR, 0.25 ** FACTOR / MOMENTUM_SCALE, 0.25 ** FACTOR / MOMENTUM_SCALE]
    square = None
    shifts = []
    for k in range(2):
        part = ext.at[k, :, :, pl.ds(HALO, rows), :]
        pltpu.make_async_copy(part, part, local_sem.at[k]).wait()
        halo_bytes(k).wait_recv()
        for f in range(3):
            for b in range(count):
                for i in range(blocks):
                    value = ext[k, f, i, pl.ds(b, SUBLANES, stride=count), :]
                    if f > 0:
                        value = value * MOMENTUM_SCALE
                    states[k, 0, f, b, :, i * LANES:(i + 1) * LANES] = value
        square = propagate(k, SQUARE_SCALE)
        for f in range(3):
            for b in range(count):
                for i in range(blocks):
                    settled[k, f, i, pl.ds(b, SUBLANES, stride=count), :] = (
                        states[k, 0, f, b, :, i * LANES:(i + 1) * LANES] * middle[f]
                    )
        if k == 0:
            back = pltpu.make_async_remote_copy(
                src_ref=settled.at[0, :, :, pl.ds(HALO, rows), :],
                dst_ref=behind.at[:, :, pl.ds(HALO, rows), :],
                send_sem=shift_send.at[0],
                recv_sem=shift_recv.at[0],
                device_id=(before, s),
                device_id_type=MESH,
            )
            back.start()
            kept = [
                pltpu.make_async_copy(
                    settled.at[0, :, i, pl.ds(HALO, rows), :], updated.at[1, :, :, lanes[i]], local_sem.at[3]
                )
                for i in range(blocks)
            ]
            for copy in kept:
                copy.start()
        else:
            onward = [
                pltpu.make_async_remote_copy(
                    src_ref=settled.at[1, :, i, pl.ds(HALO, rows), :],
                    dst_ref=updated.at[0, :, :, lanes[i]],
                    send_sem=shift_send.at[1],
                    recv_sem=shift_recv.at[1],
                    device_id=(after, s),
                    device_id_type=MESH,
                )
                for i in range(blocks)
            ]

            @pl.when(t < times - 1)
            def _():
                for copy in onward:
                    copy.start()

    def row_copy(k, j):
        interval = lax.rem(2 * t + 1 + k, 2 * times)
        return (
            stage.at[k, pl.ds((HALO + j) * 3, 3)],
            coarse.at[pl.ds(interval * 3, 3)],
        )

    for k in range(2):
        propagate(k, square)
        if k == 1:
            back.wait_recv()
        wrapped = t == times - 1
        for b in range(count):
            for f in range(3):
                for i in range(blocks):
                    value = states[k, 0, f, b, :, i * LANES:(i + 1) * LANES] * down[f]
                    if k == 0:
                        known = settled[1, f, i, pl.ds(b, SUBLANES, stride=count), :]
                    else:
                        known = behind[f, i, pl.ds(b, SUBLANES, stride=count), :]
                        value = jnp.where(wrapped, known, value)
                    stage[k, pl.ds(b * 3 + f, SUBLANES, stride=3 * count), i, :] = value - known

        @pl.loop(1, times)
        def _(d):
            j = lax.rem(t + d, times)
            source, place = row_copy(k, j)
            pltpu.make_async_remote_copy(
                src_ref=source, dst_ref=place, send_sem=row_send.at[k], recv_sem=row_recv.at[k],
                device_id=(j, s), device_id_type=MESH,
            ).start()

        source, place = row_copy(k, t)
        pltpu.make_async_copy(source, place, local_sem.at[4 + k]).start()

    for k in range(2):
        halo_bytes(k).wait_send()
    back.wait_send()
    pltpu.make_async_copy(updated.at[1], updated.at[1], local_sem.at[3]).wait()
    whole = pltpu.make_async_remote_copy(
        src_ref=updated.at[0], dst_ref=updated.at[0], send_sem=shift_send.at[1], recv_sem=shift_recv.at[1],
        device_id=(after, s), device_id_type=MESH,
    )

    @pl.when(t == 0)
    def _():
        opening.wait()

    @pl.when(t > 0)
    def _():
        whole.wait_recv()

    @pl.when(t < times - 1)
    def _():
        whole.wait_send()

    for k in range(2):
        part = coarse.at[pl.ds(0, 3 * (times - 1))]
        total = pltpu.make_async_remote_copy(
            src_ref=part, dst_ref=part, send_sem=row_send.at[k], recv_sem=row_recv.at[k],
            device_id=(after, s), device_id_type=MESH,
        )
        total.wait_recv()
        total.wait_send()
        source, place = row_copy(k, t)
        pltpu.make_async_copy(source, place, local_sem.at[4 + k]).wait()


def solution(mesh):
    def on_device(c_points):
        intervals, fields, rows, columns = c_points.shape
        times = lax.axis_size("tm")
        blocks = columns // LANES
        full = rows + 2 * HALO
        f32 = jnp.float32
        updated, coarse = pl.pallas_call(
            kernel,
            out_shape=(
                jax.ShapeDtypeStruct(c_points.shape, f32),
                jax.ShapeDtypeStruct((2 * times * fields, blocks, LANES), f32),
            ),
            in_specs=[pl.BlockSpec(memory_space=pl.ANY)],
            out_specs=(pl.BlockSpec(memory_space=pl.ANY), pl.BlockSpec(memory_space=pl.ANY)),
            scratch_shapes=[
                pltpu.VMEM((2, fields, blocks, full, LANES), f32),
                pltpu.VMEM((2, 2, fields, full // SUBLANES, SUBLANES, columns), f32),
                pltpu.VMEM((2, fields, blocks, full, LANES), f32),
                pltpu.VMEM((fields, blocks, full, LANES), f32),
                pltpu.VMEM((2, full * fields, blocks, LANES), f32),
                pltpu.SemaphoreType.DMA((6,)),
                pltpu.SemaphoreType.DMA((2,)),
                pltpu.SemaphoreType.DMA((2,)),
                pltpu.SemaphoreType.DMA((2,)),
                pltpu.SemaphoreType.DMA((2,)),
                pltpu.SemaphoreType.DMA((2,)),
                pltpu.SemaphoreType.DMA((2,)),
            ],
            compiler_params=pltpu.CompilerParams(collective_id=0, has_side_effects=True),
        )(c_points)
        return updated, coarse.reshape(2 * times, fields, 1, 1, columns)

    return jax.shard_map(
        on_device,
        mesh=mesh,
        in_specs=(P("tm", None, "space", None),),
        out_specs=(P("tm", None, "space", None), P(None, None, "space", "tm", None)),
        check_vma=False,
    )
```

```python
import jax
import jax.numpy as jnp
from jax import lax
from jax.experimental import pallas as pl
from jax.experimental.pallas import tpu as pltpu
from jax.sharding import PartitionSpec as P

FACTOR = 8
LANES = 128
HALO = 2 * FACTOR
SUBLANES = 8
MOMENTUM_SCALE = 0.4
SQUARE_SCALE = 0.08
SCALE_BACK = [0.25 ** FACTOR, 0.25 ** FACTOR / MOMENTUM_SCALE, 0.25 ** FACTOR / MOMENTUM_SCALE]
RUN = 4
MESH = pl.DeviceIdType.MESH


def inverse(height):
    return 1.0 / height


def step_rows(src, dst, square):
    count = src.shape[1]
    columns = src.shape[3]

    def parts(b):
        h, p, q = src[0, b], src[1, b], src[2, b]
        r = inverse(h)
        u = p * r
        v = q * r
        mixed = u * q
        half = (h * square) * h
        east = u * p + half
        north = v * q + half
        from_east = (h - p, p - east, q - mixed)
        from_west = (h + p, p + east, q + mixed)
        from_north = (h - q, p - mixed, q - north)
        from_south = (h + q, p + mixed, q + north)
        across = [
            pltpu.roll(e, columns - 1, axis=1) + pltpu.roll(w, 1, axis=1)
            for e, w in zip(from_east, from_west)
        ]
        return across, from_north, from_south

    def put(b, across, north, south):
        for f in range(3):
            dst[f, b] = across[f] + (north[f] + south[f])

    first = parts(0)
    second = parts(1)
    older, old = first, second
    for b in range(2, count):
        new = parts(b)
        put(b - 1, old[0], new[1], older[2])
        older, old = old, new
    put(count - 1, old[0], [pltpu.roll(x, SUBLANES - 1, axis=0) for x in first[1]], older[2])
    put(0, first[0], second[1], [pltpu.roll(x, 1, axis=0) for x in old[2]])


def kernel(c_ref, updated, coarse, ext, states, settled, behind, stage,
           local_sem, halo_send, halo_recv, back_send, back_recv, on_send, on_recv, row_send, row_recv):
    t = lax.axis_index("tm")
    s = lax.axis_index("space")
    times = lax.axis_size("tm")
    strips = lax.axis_size("space")
    rows, columns = c_ref.shape[2], c_ref.shape[3]
    blocks = columns // LANES
    half = rows // 2
    wide = half + 2 * HALO
    narrow = half + 2 * FACTOR
    low = lax.rem(s + strips - 1, strips)
    high = lax.rem(s + 1, strips)
    before = lax.rem(t + times - 1, times)
    after = lax.rem(t + 1, times)

    barrier = pltpu.get_barrier_semaphore()
    for neighbour in (low, high):
        pl.semaphore_signal(barrier, inc=1, device_id=(t, neighbour), device_id_type=MESH)

    @pl.loop(1, times)
    def _(d):
        pl.semaphore_signal(barrier, inc=1, device_id=(lax.rem(t + d, times), s), device_id_type=MESH)

    lanes = [pl.ds(i * LANES, LANES) for i in range(blocks)]
    for k in range(2):
        for i in range(blocks):
            pltpu.make_async_copy(
                c_ref.at[k, :, :, lanes[i]], ext.at[k, :, i, pl.ds(HALO, rows), :], local_sem.at[k]
            ).start()
    opening = pltpu.make_async_copy(c_ref.at[0], updated.at[0], local_sem.at[2])

    @pl.when(t == 0)
    def _():
        opening.start()

    pl.semaphore_wait(barrier, times + 1)

    def halo_copy(side, k, source, target):
        return pltpu.make_async_remote_copy(
            src_ref=source, dst_ref=target, send_sem=halo_send.at[side, k], recv_sem=halo_recv.at[side, k],
            device_id=(t, low if side else high), device_id_type=MESH,
        )

    for k in range(2):
        for i in range(blocks):
            for side, source, place in ((0, rows - HALO, 0), (1, 0, HALO + rows)):
                halo_copy(
                    side, k,
                    c_ref.at[k, :, pl.ds(source, HALO), lanes[i]],
                    ext.at[k, :, i, pl.ds(place, HALO), :],
                ).start()

    def halo_bytes(side, k):
        part = ext.at[k, :, :, pl.ds(0, HALO), :]
        return pltpu.make_async_remote_copy(
            src_ref=part, dst_ref=part, send_sem=halo_send.at[side, k], recv_sem=halo_recv.at[side, k],
            device_id=(t, high), device_id_type=MESH,
        )

    def propagate(load, count):
        a = states.at[0, :, pl.ds(0, count)]
        b = states.at[1, :, pl.ds(0, count)]
        for f in range(3):
            for r in range(count):
                for i in range(blocks):
                    value = load(f, i, r, count)
                    a[f, r, :, i * LANES:(i + 1) * LANES] = value if f == 0 else value * MOMENTUM_SCALE

        def two(_, square):
            step_rows(a, b, square)
            square = square * 0.25
            step_rows(b, a, square)
            return square * 0.25

        lax.fori_loop(0, FACTOR // 2, two, SQUARE_SCALE)
        return lambda f, i, r: a[f, r, :, i * LANES:(i + 1) * LANES] * SCALE_BACK[f]

    flip = (lax.rem(s, RUN) == 0).astype(jnp.int32)
    center = pl.ds(HALO, half)
    wrapped = t == times - 1

    def own_copy(w, offset):
        return [
            pltpu.make_async_copy(
                settled.at[w, 0, :, i, center, :], updated.at[1, :, pl.ds(offset, half), lanes[i]], local_sem.at[3]
            )
            for i in range(blocks)
        ]

    def back_copy(w):
        return pltpu.make_async_remote_copy(
            src_ref=settled.at[w, 0, :, :, center, :], dst_ref=behind.at[w, :, :, pl.ds(FACTOR, half), :],
            send_sem=back_send.at[w], recv_sem=back_recv.at[w], device_id=(before, s), device_id_type=MESH,
        )

    def on_copy(w, offset):
        return [
            pltpu.make_async_remote_copy(
                src_ref=settled.at[w, 1, :, i, center, :], dst_ref=updated.at[0, :, pl.ds(offset, half), lanes[i]],
                send_sem=on_send, recv_sem=on_recv, device_id=(after, s), device_id_type=MESH,
            )
            for i in range(blocks)
        ]

    def send_rows(w, k, offset):
        place = coarse.at[pl.ds(lax.rem(2 * t + 1 + k, 2 * times) * 3, 3)]

        @pl.loop(0, half)
        def _(d):
            row = lax.rem(t + d, half)
            j = offset + row
            source = stage.at[w, k, pl.ds((FACTOR + row) * 3, 3)]

            @pl.when(j != t)
            def _():
                pltpu.make_async_remote_copy(
                    src_ref=source, dst_ref=place, send_sem=row_send.at[k], recv_sem=row_recv.at[k],
                    device_id=(j, s), device_id_type=MESH,
                ).start()

            @pl.when(j == t)
            def _():
                pltpu.make_async_copy(source, place, local_sem.at[4 + k]).start()

    @pl.loop(0, 2)
    def _(w):
        side = lax.rem(w + flip, 2)
        offset = pl.multiple_of(side * half, SUBLANES)

        def advance(k):
            @pl.when(w == 0)
            def _():
                part = ext.at[k, :, :, pl.ds(HALO, rows), :]
                pltpu.make_async_copy(part, part, local_sem.at[k]).wait()

            halo_bytes(side, k).wait_recv()
            result = propagate(
                lambda f, i, r, count: ext[k, f, i, pl.ds(offset + r, SUBLANES, stride=count), :],
                wide // SUBLANES,
            )
            for f in range(3):
                for r in range(wide // SUBLANES):
                    for i in range(blocks):
                        settled[w, k, f, i, pl.ds(r, SUBLANES, stride=wide // SUBLANES), :] = result(f, i, r)

        def push(k):
            return propagate(
                lambda f, i, r, count: settled[w, k, f, i, pl.ds(FACTOR + r, SUBLANES, stride=count), :],
                narrow // SUBLANES,
            )

        def residual(k, result):
            count = narrow // SUBLANES
            for f in range(3):
                for r in range(count):
                    for i in range(blocks):
                        value = result(f, i, r)
                        if k == 0:
                            known = settled[w, 1, f, i, pl.ds(FACTOR + r, SUBLANES, stride=count), :]
                        else:
                            known = behind[w, f, i, pl.ds(r, SUBLANES, stride=count), :]
                            value = jnp.where(wrapped, known, value)
                        stage[w, k, pl.ds(r * 3 + f, SUBLANES, stride=3 * count), i, :] = value - known

        advance(0)
        back_copy(w).start()
        for copy in own_copy(w, offset):
            copy.start()
        result = push(0)
        for f in range(3):
            for r in range(narrow // SUBLANES):
                for i in range(blocks):
                    pushed_value = result(f, i, r)
                    stage[w, 0, pl.ds(r * 3 + f, SUBLANES, stride=3 * (narrow // SUBLANES)), i, :] = pushed_value
        advance(1)

        @pl.when(t < times - 1)
        def _():
            for copy in on_copy(w, offset):
                copy.start()

        count = narrow // SUBLANES
        residual(0, lambda f, i, r: stage[w, 0, pl.ds(r * 3 + f, SUBLANES, stride=3 * count), i, :])
        send_rows(w, 0, offset)
        result = push(1)
        back_copy(w).wait_recv()
        residual(1, result)
        send_rows(w, 1, offset)

    for k in range(2):
        for side in range(2):
            halo_bytes(side, k).wait_send()
    for w in range(2):
        back_copy(w).wait_send()
    pltpu.make_async_copy(updated.at[1], updated.at[1], local_sem.at[3]).wait()
    whole = pltpu.make_async_remote_copy(
        src_ref=updated.at[0], dst_ref=updated.at[0], send_sem=on_send, recv_sem=on_recv,
        device_id=(after, s), device_id_type=MESH,
    )

    @pl.when(t == 0)
    def _():
        opening.wait()

    @pl.when(t > 0)
    def _():
        whole.wait_recv()

    @pl.when(t < times - 1)
    def _():
        whole.wait_send()

    for k in range(2):
        part = coarse.at[pl.ds(0, 3 * (times - 1))]
        total = pltpu.make_async_remote_copy(
            src_ref=part, dst_ref=part, send_sem=row_send.at[k], recv_sem=row_recv.at[k],
            device_id=(after, s), device_id_type=MESH,
        )
        total.wait_recv()
        total.wait_send()
        one = coarse.at[pl.ds(0, 3)]
        pltpu.make_async_copy(one, one, local_sem.at[4 + k]).wait()


def solution(mesh):
    def on_device(c_points):
        intervals, fields, rows, columns = c_points.shape
        times = lax.axis_size("tm")
        blocks = columns // LANES
        full = rows + 2 * HALO
        wide = rows // 2 + 2 * HALO
        narrow = rows // 2 + 2 * FACTOR
        f32 = jnp.float32
        updated, coarse = pl.pallas_call(
            kernel,
            out_shape=(
                pltpu.VMEM(c_points.shape, f32),
                pltpu.VMEM((2 * times * fields, blocks, LANES), f32),
            ),
            in_specs=[pl.BlockSpec(memory_space=pl.ANY)],
            out_specs=(pl.BlockSpec(memory_space=pltpu.VMEM), pl.BlockSpec(memory_space=pltpu.VMEM)),
            scratch_shapes=[
                pltpu.VMEM((2, fields, blocks, full, LANES), f32),
                pltpu.VMEM((2, fields, wide // SUBLANES, SUBLANES, columns), f32),
                pltpu.VMEM((2, 2, fields, blocks, wide, LANES), f32),
                pltpu.VMEM((2, fields, blocks, narrow, LANES), f32),
                pltpu.VMEM((2, 2, narrow * fields, blocks, LANES), f32),
                pltpu.SemaphoreType.DMA((6,)),
                pltpu.SemaphoreType.DMA((2, 2)),
                pltpu.SemaphoreType.DMA((2, 2)),
                pltpu.SemaphoreType.DMA((2,)),
                pltpu.SemaphoreType.DMA((2,)),
                pltpu.SemaphoreType.DMA,
                pltpu.SemaphoreType.DMA,
                pltpu.SemaphoreType.DMA((2,)),
                pltpu.SemaphoreType.DMA((2,)),
            ],
            compiler_params=pltpu.CompilerParams(collective_id=0, has_side_effects=True),
        )(c_points)
        return updated, coarse.reshape(2 * times, fields, 1, 1, columns)

    return jax.shard_map(
        on_device,
        mesh=mesh,
        in_specs=(P("tm", None, "space", None),),
        out_specs=(P("tm", None, "space", None), P(None, None, "space", "tm", None)),
        check_vma=False,
    )
```

```python
import jax
import jax.numpy as jnp
from jax import lax
from jax.experimental import pallas as pl
from jax.experimental.pallas import tpu as pltpu
from jax.sharding import PartitionSpec as P

FACTOR = 8
LANES = 128
HALO = 2 * FACTOR
SUBLANES = 8
MOMENTUM_SCALE = 0.4
SQUARE_SCALE = 0.08
SCALE_BACK = [0.25 ** FACTOR, 0.25 ** FACTOR / MOMENTUM_SCALE, 0.25 ** FACTOR / MOMENTUM_SCALE]
RUN = 4
LINE = 4
CORES = 2
MESH = pl.DeviceIdType.MESH


def inverse(height):
    return 1.0 / height


def step_rows(src, dst, square):
    count = src.shape[1]
    columns = src.shape[3]

    def parts(b):
        h, p, q = src[0, b], src[1, b], src[2, b]
        r = inverse(h)
        u = p * r
        v = q * r
        mixed = u * q
        half = (h * square) * h
        east = u * p + half
        north = v * q + half
        from_east = (h - p, p - east, q - mixed)
        from_west = (h + p, p + east, q + mixed)
        from_north = (h - q, p - mixed, q - north)
        from_south = (h + q, p + mixed, q + north)
        across = [
            pltpu.roll(e, columns - 1, axis=1) + pltpu.roll(w, 1, axis=1)
            for e, w in zip(from_east, from_west)
        ]
        return across, from_north, from_south

    def put(b, across, north, south):
        for f in range(3):
            dst[f, b] = across[f] + (north[f] + south[f])

    first = parts(0)
    second = parts(1)
    older, old = first, second
    for b in range(2, count):
        new = parts(b)
        put(b - 1, old[0], new[1], older[2])
        older, old = old, new
    put(count - 1, old[0], [pltpu.roll(x, SUBLANES - 1, axis=0) for x in first[1]], older[2])
    put(0, first[0], second[1], [pltpu.roll(x, 1, axis=0) for x in old[2]])


def kernel(c_ref, updated, coarse, ext, relay, states, settled, behind, stage,
           local_sem, halo_send, halo_recv, back_send, back_recv, on_send, on_recv, row_send, row_recv,
           relay_send, relay_recv, known_in):
    t = lax.axis_index("tm")
    s = lax.axis_index("space")
    times = lax.axis_size("tm")
    strips = lax.axis_size("space")
    rows, columns = c_ref.shape[2], c_ref.shape[3]
    blocks = columns // LANES
    half = rows // 2
    wide = half + 2 * HALO
    narrow = half + 2 * FACTOR
    low = lax.rem(s + strips - 1, strips)
    high = lax.rem(s + 1, strips)
    before = lax.rem(t + times - 1, times)
    after = lax.rem(t + 1, times)

    spot = lax.rem(s, RUN)
    ending = spot == RUN - 1
    starting = spot == 0
    outer = jnp.logical_or(ending, starting)
    inner = jnp.logical_not(outer)
    upward = (spot < 2).astype(jnp.int32)
    leads = jnp.logical_and(outer, s < strips // 2)
    follows = jnp.logical_and(outer, s >= strips // 2)
    distant = jnp.where(upward == 1, low, high)
    beyond = lax.rem(s + strips + 2 - 4 * upward, strips)

    plane = LINE * CORES
    place_in_line = lax.rem(t // CORES, LINE)
    partner = t + 1 - 2 * lax.rem(t, CORES)
    around = (lax.rem(t + plane, times), lax.rem(t + times - plane, times))
    fore = place_in_line < LINE - 1
    aft = place_in_line > 0
    along = 1 + jnp.logical_and(fore, aft).astype(jnp.int32)
    near_pair = t + CORES * (1 - 2 * lax.rem(place_in_line, 2))
    far_pair = t + 2 * CORES * (1 - 2 * (place_in_line // 2))

    def tell(semaphore, group, strip=s):
        pl.semaphore_signal(semaphore, inc=1, device_id=(group, strip), device_id_type=MESH)

    def tell_around(semaphore):
        for group in around:
            tell(semaphore, group)

        @pl.when(fore)
        def _():
            tell(semaphore, t + CORES)

        @pl.when(aft)
        def _():
            tell(semaphore, t - CORES)

    barrier = pltpu.get_barrier_semaphore()
    @pl.when(jnp.logical_not(jnp.logical_and(follows, upward == 1)))
    def _():
        tell(barrier, t, low)

    @pl.when(jnp.logical_not(jnp.logical_and(follows, upward == 0)))
    def _():
        tell(barrier, t, high)

    tell(barrier, partner)
    tell_around(barrier)

    lanes = [pl.ds(i * LANES, LANES) for i in range(blocks)]
    for k in range(2):
        for i in range(blocks):
            pltpu.make_async_copy(
                c_ref.at[k, :, :, lanes[i]], ext.at[k, :, i, pl.ds(HALO, rows), :], local_sem.at[k]
            ).start()
    opening = pltpu.make_async_copy(c_ref.at[0], updated.at[0], local_sem.at[2])

    @pl.when(t == 0)
    def _():
        opening.start()

    pl.semaphore_wait(barrier, 5 + along - leads.astype(jnp.int32))

    def halo_copy(side, k, source, target):
        return pltpu.make_async_remote_copy(
            src_ref=source, dst_ref=target, send_sem=halo_send.at[side, k], recv_sem=halo_recv.at[side, k],
            device_id=(t, low if side else high), device_id_type=MESH,
        )

    def halo_start(side, k, source, place):
        for i in range(blocks):
            halo_copy(
                side, k,
                c_ref.at[k, :, pl.ds(source, HALO), lanes[i]],
                ext.at[k, :, i, pl.ds(place, HALO), :],
            ).start()

    def side_start(side, k):
        halo_start(side, k, 0 if side else rows - HALO, HALO + rows if side else 0)

    def far_start():
        relay_start()
        for side in range(2):

            @pl.when(upward == side)
            def _():
                side_start(side, 0)

    def relay_start():
        source = pl.multiple_of((1 - upward) * (rows - HALO), SUBLANES)
        hop = jnp.where(upward == 1, high, low)
        for i in range(blocks):
            pltpu.make_async_remote_copy(
                src_ref=c_ref.at[1, :, pl.ds(source, HALO), lanes[i]], dst_ref=relay.at[:, i],
                send_sem=halo_send.at[upward, 1], recv_sem=relay_recv,
                device_id=(t, hop), device_id_type=MESH,
            ).start()

    @pl.when(follows)
    def _():
        tell(known_in.at[4], t, distant)
        far_start()

    for k in range(2):
        for side in range(2):

            @pl.when(jnp.logical_or(inner, upward != side))
            def _():
                side_start(side, k)

    def relay_copy():
        place = pl.multiple_of(upward * (HALO + rows), SUBLANES)
        return pltpu.make_async_remote_copy(
            src_ref=relay, dst_ref=ext.at[1, :, :, pl.ds(place, HALO), :],
            send_sem=relay_send, recv_sem=halo_recv.at[upward, 1],
            device_id=(t, beyond), device_id_type=MESH,
        )

    tell_around(known_in.at[0])
    pl.semaphore_wait(known_in.at[0], 2 + along)
    for stage_index, group in ((1, near_pair), (2, far_pair), (3, partner)):
        tell(known_in.at[stage_index], group)
        pl.semaphore_wait(known_in.at[stage_index], 1)

    def forward():
        pltpu.make_async_remote_copy(
            src_ref=relay, dst_ref=relay, send_sem=relay_send, recv_sem=relay_recv,
            device_id=(t, high), device_id_type=MESH,
        ).wait_recv()
        relay_copy().start()

    @pl.when(jnp.logical_and(inner, s >= strips // 2))
    def _():
        forward()

    def halo_bytes(side, k):
        part = ext.at[k, :, :, pl.ds(0, HALO), :]
        return pltpu.make_async_remote_copy(
            src_ref=part, dst_ref=part, send_sem=halo_send.at[side, k], recv_sem=halo_recv.at[side, k],
            device_id=(t, high), device_id_type=MESH,
        )

    def propagate(load, count):
        a = states.at[0, :, pl.ds(0, count)]
        b = states.at[1, :, pl.ds(0, count)]
        for f in range(3):
            for r in range(count):
                for i in range(blocks):
                    value = load(f, i, r, count)
                    a[f, r, :, i * LANES:(i + 1) * LANES] = value if f == 0 else value * MOMENTUM_SCALE

        def two(_, square):
            step_rows(a, b, square)
            square = square * 0.25
            step_rows(b, a, square)
            return square * 0.25

        lax.fori_loop(0, FACTOR // 2, two, SQUARE_SCALE)
        return lambda f, i, r: a[f, r, :, i * LANES:(i + 1) * LANES] * SCALE_BACK[f]

    center = pl.ds(HALO, half)
    wrapped = t == times - 1

    def own_copy(w, offset):
        return [
            pltpu.make_async_copy(
                settled.at[w, 0, :, i, center, :], updated.at[1, :, pl.ds(offset, half), lanes[i]], local_sem.at[3]
            )
            for i in range(blocks)
        ]

    def back_copy(w):
        return pltpu.make_async_remote_copy(
            src_ref=settled.at[w, 0, :, :, center, :], dst_ref=behind.at[w, :, :, pl.ds(FACTOR, half), :],
            send_sem=back_send.at[w], recv_sem=back_recv.at[w], device_id=(before, s), device_id_type=MESH,
        )

    def on_copy(w, offset):
        return [
            pltpu.make_async_remote_copy(
                src_ref=settled.at[w, 1, :, i, center, :], dst_ref=updated.at[0, :, pl.ds(offset, half), lanes[i]],
                send_sem=on_send, recv_sem=on_recv, device_id=(after, s), device_id_type=MESH,
            )
            for i in range(blocks)
        ]

    def send_rows(w, k, offset):
        place = coarse.at[pl.ds(lax.rem(2 * t + 1 + k, 2 * times) * 3, 3)]

        @pl.loop(0, half)
        def _(d):
            row = lax.rem(t + d, half)
            j = offset + row
            source = stage.at[w, k, pl.ds((FACTOR + row) * 3, 3)]

            @pl.when(j != t)
            def _():
                pltpu.make_async_remote_copy(
                    src_ref=source, dst_ref=place, send_sem=row_send.at[k], recv_sem=row_recv.at[k],
                    device_id=(j, s), device_id_type=MESH,
                ).start()

            @pl.when(j == t)
            def _():
                pltpu.make_async_copy(source, place, local_sem.at[4 + k]).start()

    @pl.loop(0, 2)
    def _(w):
        side = lax.rem(w + upward, 2)
        offset = pl.multiple_of(side * half, SUBLANES)

        def advance(k):
            @pl.when(w == 0)
            def _():
                part = ext.at[k, :, :, pl.ds(HALO, rows), :]
                pltpu.make_async_copy(part, part, local_sem.at[k]).wait()

            halo_bytes(side, k).wait_recv()
            result = propagate(
                lambda f, i, r, count: ext[k, f, i, pl.ds(offset + r, SUBLANES, stride=count), :],
                wide // SUBLANES,
            )
            for f in range(3):
                for r in range(wide // SUBLANES):
                    for i in range(blocks):
                        settled[w, k, f, i, pl.ds(r, SUBLANES, stride=wide // SUBLANES), :] = result(f, i, r)

        def push(k):
            return propagate(
                lambda f, i, r, count: settled[w, k, f, i, pl.ds(FACTOR + r, SUBLANES, stride=count), :],
                narrow // SUBLANES,
            )

        def residual(k, result):
            count = narrow // SUBLANES
            for f in range(3):
                for r in range(count):
                    for i in range(blocks):
                        value = result(f, i, r)
                        if k == 0:
                            known = settled[w, 1, f, i, pl.ds(FACTOR + r, SUBLANES, stride=count), :]
                        else:
                            known = behind[w, f, i, pl.ds(r, SUBLANES, stride=count), :]
                            value = jnp.where(wrapped, known, value)
                        stage[w, k, pl.ds(r * 3 + f, SUBLANES, stride=3 * count), i, :] = value - known

        @pl.when(jnp.logical_and(w == 1, jnp.logical_and(inner, s < strips // 2)))
        def _():
            forward()

        advance(0)

        @pl.when(jnp.logical_and(w == 0, leads))
        def _():
            pl.semaphore_wait(known_in.at[4], 1)
            far_start()

        back_copy(w).start()
        for copy in own_copy(w, offset):
            copy.start()
        result = push(0)
        for f in range(3):
            for r in range(narrow // SUBLANES):
                for i in range(blocks):
                    pushed_value = result(f, i, r)
                    stage[w, 0, pl.ds(r * 3 + f, SUBLANES, stride=3 * (narrow // SUBLANES)), i, :] = pushed_value

        advance(1)

        @pl.when(t < times - 1)
        def _():
            for copy in on_copy(w, offset):
                copy.start()

        count = narrow // SUBLANES
        residual(0, lambda f, i, r: stage[w, 0, pl.ds(r * 3 + f, SUBLANES, stride=3 * count), i, :])
        send_rows(w, 0, offset)
        result = push(1)
        back_copy(w).wait_recv()
        residual(1, result)
        send_rows(w, 1, offset)

    for k in range(2):
        for side in range(2):
            halo_bytes(side, k).wait_send()
    for w in range(2):
        back_copy(w).wait_send()

    @pl.when(inner)
    def _():
        relay_copy().wait_send()

    pltpu.make_async_copy(updated.at[1], updated.at[1], local_sem.at[3]).wait()
    whole = pltpu.make_async_remote_copy(
        src_ref=updated.at[0], dst_ref=updated.at[0], send_sem=on_send, recv_sem=on_recv,
        device_id=(after, s), device_id_type=MESH,
    )

    @pl.when(t == 0)
    def _():
        opening.wait()

    @pl.when(t > 0)
    def _():
        whole.wait_recv()

    @pl.when(t < times - 1)
    def _():
        whole.wait_send()

    for k in range(2):
        part = coarse.at[pl.ds(0, 3 * (times - 1))]
        total = pltpu.make_async_remote_copy(
            src_ref=part, dst_ref=part, send_sem=row_send.at[k], recv_sem=row_recv.at[k],
            device_id=(after, s), device_id_type=MESH,
        )
        total.wait_recv()
        total.wait_send()
        one = coarse.at[pl.ds(0, 3)]
        pltpu.make_async_copy(one, one, local_sem.at[4 + k]).wait()


def solution(mesh):
    def on_device(c_points):
        intervals, fields, rows, columns = c_points.shape
        times = lax.axis_size("tm")
        blocks = columns // LANES
        full = rows + 2 * HALO
        wide = rows // 2 + 2 * HALO
        narrow = rows // 2 + 2 * FACTOR
        f32 = jnp.float32
        updated, coarse = pl.pallas_call(
            kernel,
            out_shape=(
                pltpu.VMEM(c_points.shape, f32),
                pltpu.VMEM((2 * times * fields, blocks, LANES), f32),
            ),
            in_specs=[pl.BlockSpec(memory_space=pl.ANY)],
            out_specs=(pl.BlockSpec(memory_space=pltpu.VMEM), pl.BlockSpec(memory_space=pltpu.VMEM)),
            scratch_shapes=[
                pltpu.VMEM((2, fields, blocks, full, LANES), f32),
                pltpu.VMEM((fields, blocks, HALO, LANES), f32),
                pltpu.VMEM((2, fields, wide // SUBLANES, SUBLANES, columns), f32),
                pltpu.VMEM((2, 2, fields, blocks, wide, LANES), f32),
                pltpu.VMEM((2, fields, blocks, narrow, LANES), f32),
                pltpu.VMEM((2, 2, narrow * fields, blocks, LANES), f32),
                pltpu.SemaphoreType.DMA((6,)),
                pltpu.SemaphoreType.DMA((2, 2)),
                pltpu.SemaphoreType.DMA((2, 2)),
                pltpu.SemaphoreType.DMA((2,)),
                pltpu.SemaphoreType.DMA((2,)),
                pltpu.SemaphoreType.DMA,
                pltpu.SemaphoreType.DMA,
                pltpu.SemaphoreType.DMA((2,)),
                pltpu.SemaphoreType.DMA((2,)),
                pltpu.SemaphoreType.DMA,
                pltpu.SemaphoreType.DMA,
                pltpu.SemaphoreType.REGULAR((5,)),
            ],
            compiler_params=pltpu.CompilerParams(collective_id=0, has_side_effects=True),
        )(c_points)
        return updated, coarse.reshape(2 * times, fields, 1, 1, columns)

    return jax.shard_map(
        on_device,
        mesh=mesh,
        in_specs=(P("tm", None, "space", None),),
        out_specs=(P("tm", None, "space", None), P(None, None, "space", "tm", None)),
        check_vma=False,
    )
```

```python
import jax
import jax.numpy as jnp
from jax import lax
from jax.experimental import pallas as pl
from jax.experimental.pallas import tpu as pltpu
from jax.sharding import PartitionSpec as P

FACTOR = 8
LANES = 128
HALO = 2 * FACTOR
SUBLANES = 8
MOMENTUM_SCALE = 0.4
SQUARE_SCALE = 0.08
SCALE_BACK = [0.25 ** FACTOR, 0.25 ** FACTOR / MOMENTUM_SCALE, 0.25 ** FACTOR / MOMENTUM_SCALE]
RUN = 4
LINE = 4
CORES = 2
MESH = pl.DeviceIdType.MESH


def inverse(height):
    return 1.0 / height


def step_rows(src, dst, square):
    count = src.shape[1]
    columns = src.shape[3]

    def parts(b):
        h, p, q = src[0, b], src[1, b], src[2, b]
        r = inverse(h)
        u = p * r
        v = q * r
        mixed = u * q
        half = (h * square) * h
        east = u * p + half
        north = v * q + half
        from_east = (h - p, p - east, q - mixed)
        from_west = (h + p, p + east, q + mixed)
        from_north = (h - q, p - mixed, q - north)
        from_south = (h + q, p + mixed, q + north)
        across = [
            pltpu.roll(e, columns - 1, axis=1) + pltpu.roll(w, 1, axis=1)
            for e, w in zip(from_east, from_west)
        ]
        return across, from_north, from_south

    def put(b, across, north, south):
        for f in range(3):
            dst[f, b] = across[f] + (north[f] + south[f])

    first = parts(0)
    second = parts(1)
    older, old = first, second
    for b in range(2, count):
        new = parts(b)
        put(b - 1, old[0], new[1], older[2])
        older, old = old, new
    put(count - 1, old[0], [pltpu.roll(x, SUBLANES - 1, axis=0) for x in first[1]], older[2])
    put(0, first[0], second[1], [pltpu.roll(x, 1, axis=0) for x in old[2]])


def kernel(c_ref, arrived, settled, coarse, ext, relay, states, pushed, behind, stage,
           local_sem, halo_send, halo_recv, back_send, back_recv, on_send, on_recv, row_send, row_recv,
           relay_send, relay_recv, known_in):
    t = lax.axis_index("tm")
    s = lax.axis_index("space")
    times = lax.axis_size("tm")
    strips = lax.axis_size("space")
    rows, columns = c_ref.shape[2], c_ref.shape[3]
    blocks = columns // LANES
    half = rows // 2
    wide = half + 2 * HALO
    narrow = half + 2 * FACTOR
    low = lax.rem(s + strips - 1, strips)
    high = lax.rem(s + 1, strips)
    before = lax.rem(t + times - 1, times)
    after = lax.rem(t + 1, times)

    spot = lax.rem(s, RUN)
    ending = spot == RUN - 1
    starting = spot == 0
    outer = jnp.logical_or(ending, starting)
    inner = jnp.logical_not(outer)
    upward = (spot < 2).astype(jnp.int32)
    leads = jnp.logical_and(outer, s < strips // 2)
    follows = jnp.logical_and(outer, s >= strips // 2)
    distant = jnp.where(upward == 1, low, high)
    beyond = lax.rem(s + strips + 2 - 4 * upward, strips)

    plane = LINE * CORES
    place_in_line = lax.rem(t // CORES, LINE)
    partner = t + 1 - 2 * lax.rem(t, CORES)
    around = (lax.rem(t + plane, times), lax.rem(t + times - plane, times))
    fore = place_in_line < LINE - 1
    aft = place_in_line > 0
    along = 1 + jnp.logical_and(fore, aft).astype(jnp.int32)
    near_pair = t + CORES * (1 - 2 * lax.rem(place_in_line, 2))
    far_pair = t + 2 * CORES * (1 - 2 * (place_in_line // 2))

    def tell(semaphore, group, strip=s):
        pl.semaphore_signal(semaphore, inc=1, device_id=(group, strip), device_id_type=MESH)

    def tell_around(semaphore):
        for group in around:
            tell(semaphore, group)

        @pl.when(fore)
        def _():
            tell(semaphore, t + CORES)

        @pl.when(aft)
        def _():
            tell(semaphore, t - CORES)

    barrier = pltpu.get_barrier_semaphore()
    @pl.when(jnp.logical_not(jnp.logical_and(follows, upward == 1)))
    def _():
        tell(barrier, t, low)

    @pl.when(jnp.logical_not(jnp.logical_and(follows, upward == 0)))
    def _():
        tell(barrier, t, high)

    tell(barrier, partner)
    tell_around(barrier)

    lanes = [pl.ds(i * LANES, LANES) for i in range(blocks)]
    for k in range(2):
        for i in range(blocks):
            pltpu.make_async_copy(
                c_ref.at[k, :, :, lanes[i]], ext.at[k, :, i, pl.ds(HALO, rows), :], local_sem.at[k]
            ).start()
    opening = [
        pltpu.make_async_copy(c_ref.at[0, :, :, lanes[i]], arrived.at[:, i], local_sem.at[2]) for i in range(blocks)
    ]

    @pl.when(t == 0)
    def _():
        for copy in opening:
            copy.start()

    pl.semaphore_wait(barrier, 5 + along - leads.astype(jnp.int32))

    def halo_copy(side, k, source, target):
        return pltpu.make_async_remote_copy(
            src_ref=source, dst_ref=target, send_sem=halo_send.at[side, k], recv_sem=halo_recv.at[side, k],
            device_id=(t, low if side else high), device_id_type=MESH,
        )

    def halo_start(side, k, source, place):
        for i in range(blocks):
            halo_copy(
                side, k,
                c_ref.at[k, :, pl.ds(source, HALO), lanes[i]],
                ext.at[k, :, i, pl.ds(place, HALO), :],
            ).start()

    def side_start(side, k):
        halo_start(side, k, 0 if side else rows - HALO, HALO + rows if side else 0)

    def far_start():
        relay_start()
        for side in range(2):

            @pl.when(upward == side)
            def _():
                side_start(side, 0)

    def relay_start():
        source = pl.multiple_of((1 - upward) * (rows - HALO), SUBLANES)
        hop = jnp.where(upward == 1, high, low)
        for i in range(blocks):
            pltpu.make_async_remote_copy(
                src_ref=c_ref.at[1, :, pl.ds(source, HALO), lanes[i]], dst_ref=relay.at[:, i],
                send_sem=halo_send.at[upward, 1], recv_sem=relay_recv,
                device_id=(t, hop), device_id_type=MESH,
            ).start()

    @pl.when(follows)
    def _():
        tell(known_in.at[4], t, distant)
        far_start()

    for k in range(2):
        for side in range(2):

            @pl.when(jnp.logical_or(inner, upward != side))
            def _():
                side_start(side, k)

    def relay_copy():
        place = pl.multiple_of(upward * (HALO + rows), SUBLANES)
        return pltpu.make_async_remote_copy(
            src_ref=relay, dst_ref=ext.at[1, :, :, pl.ds(place, HALO), :],
            send_sem=relay_send, recv_sem=halo_recv.at[upward, 1],
            device_id=(t, beyond), device_id_type=MESH,
        )

    tell_around(known_in.at[0])
    pl.semaphore_wait(known_in.at[0], 2 + along)
    for stage_index, group in ((1, near_pair), (2, far_pair), (3, partner)):
        tell(known_in.at[stage_index], group)
        pl.semaphore_wait(known_in.at[stage_index], 1)

    def forward():
        pltpu.make_async_remote_copy(
            src_ref=relay, dst_ref=relay, send_sem=relay_send, recv_sem=relay_recv,
            device_id=(t, high), device_id_type=MESH,
        ).wait_recv()
        relay_copy().start()

    @pl.when(jnp.logical_and(inner, s >= strips // 2))
    def _():
        forward()

    def halo_bytes(side, k):
        part = ext.at[k, :, :, pl.ds(0, HALO), :]
        return pltpu.make_async_remote_copy(
            src_ref=part, dst_ref=part, send_sem=halo_send.at[side, k], recv_sem=halo_recv.at[side, k],
            device_id=(t, high), device_id_type=MESH,
        )

    def propagate(load, count, buffers):
        a = buffers.at[0, :, pl.ds(0, count)]
        b = buffers.at[1, :, pl.ds(0, count)]
        for f in range(3):
            for r in range(count):
                for i in range(blocks):
                    value = load(f, i, r, count)
                    a[f, r, :, i * LANES:(i + 1) * LANES] = value if f == 0 else value * MOMENTUM_SCALE

        def two(_, square):
            step_rows(a, b, square)
            square = square * 0.25
            step_rows(b, a, square)
            return square * 0.25

        lax.fori_loop(0, FACTOR // 2, two, SQUARE_SCALE)
        return lambda f, i, r: a[f, r, :, i * LANES:(i + 1) * LANES] * SCALE_BACK[f]

    center = pl.ds(HALO, half)
    wrapped = t == times - 1

    def back_copy(w):
        return pltpu.make_async_remote_copy(
            src_ref=settled.at[w, 0, :, :, center, :], dst_ref=behind.at[w, :, :, pl.ds(FACTOR, half), :],
            send_sem=back_send.at[w], recv_sem=back_recv.at[w], device_id=(before, s), device_id_type=MESH,
        )

    def on_copy(w, offset):
        return pltpu.make_async_remote_copy(
            src_ref=settled.at[w, 1, :, :, center, :], dst_ref=arrived.at[:, :, pl.ds(offset, half), :],
            send_sem=on_send, recv_sem=on_recv, device_id=(after, s), device_id_type=MESH,
        )

    def send_rows(w, k, offset):
        place = coarse.at[pl.ds(lax.rem(2 * t + 1 + k, 2 * times) * 3, 3)]

        def row_copy(row):
            return pltpu.make_async_remote_copy(
                src_ref=stage.at[w, k, pl.ds((FACTOR + row) * 3, 3)], dst_ref=place,
                send_sem=row_send.at[k], recv_sem=row_recv.at[k],
                device_id=(offset + row, s), device_id_type=MESH,
            )

        @pl.loop(1, half)
        def _(d):
            row_copy(lax.rem(t + d, half)).start()

        last = lax.rem(t, half)

        @pl.when(offset + last != t)
        def _():
            row_copy(last).start()

        @pl.when(offset + last == t)
        def _():
            pltpu.make_async_copy(stage.at[w, k, pl.ds((FACTOR + last) * 3, 3)], place, local_sem.at[3 + k]).start()

    @pl.loop(0, 2)
    def _(w):
        side = lax.rem(w + upward, 2)
        offset = pl.multiple_of(side * half, SUBLANES)

        def advance(k):
            @pl.when(w == 0)
            def _():
                part = ext.at[k, :, :, pl.ds(HALO, rows), :]
                pltpu.make_async_copy(part, part, local_sem.at[k]).wait()

            halo_bytes(side, k).wait_recv()
            result = propagate(
                lambda f, i, r, count: ext[k, f, i, pl.ds(offset + r, SUBLANES, stride=count), :],
                wide // SUBLANES, states,
            )
            for f in range(3):
                for r in range(wide // SUBLANES):
                    for i in range(blocks):
                        settled[side, k, f, i, pl.ds(r, SUBLANES, stride=wide // SUBLANES), :] = result(f, i, r)

        def push(k, buffers):
            return propagate(
                lambda f, i, r, count: settled[side, k, f, i, pl.ds(FACTOR + r, SUBLANES, stride=count), :],
                narrow // SUBLANES, buffers,
            )

        def residual(k, result):
            count = narrow // SUBLANES
            for f in range(3):
                for r in range(count):
                    for i in range(blocks):
                        value = result(f, i, r)
                        if k == 0:
                            known = settled[side, 1, f, i, pl.ds(FACTOR + r, SUBLANES, stride=count), :]
                        else:
                            known = behind[side, f, i, pl.ds(r, SUBLANES, stride=count), :]
                            value = jnp.where(wrapped, known, value)
                        stage[side, k, pl.ds(r * 3 + f, SUBLANES, stride=3 * count), i, :] = value - known

        @pl.when(jnp.logical_and(w == 1, jnp.logical_and(inner, s < strips // 2)))
        def _():
            forward()

        advance(0)

        @pl.when(jnp.logical_and(w == 0, leads))
        def _():
            pl.semaphore_wait(known_in.at[4], 1)
            far_start()

        back_copy(side).start()
        first = push(0, pushed)
        advance(1)

        @pl.when(t < times - 1)
        def _():
            on_copy(side, offset).start()

        residual(0, first)
        send_rows(side, 0, offset)
        second = push(1, states)
        back_copy(side).wait_recv()
        residual(1, second)
        send_rows(side, 1, offset)

    for k in range(2):
        for side in range(2):
            halo_bytes(side, k).wait_send()
    for w in range(2):
        back_copy(w).wait_send()

    @pl.when(inner)
    def _():
        relay_copy().wait_send()

    whole = pltpu.make_async_remote_copy(
        src_ref=arrived, dst_ref=arrived, send_sem=on_send, recv_sem=on_recv,
        device_id=(after, s), device_id_type=MESH,
    )

    @pl.when(t == 0)
    def _():
        pltpu.make_async_copy(arrived, arrived, local_sem.at[2]).wait()

    @pl.when(t > 0)
    def _():
        whole.wait_recv()

    @pl.when(t < times - 1)
    def _():
        whole.wait_send()

    for k in range(2):
        part = coarse.at[pl.ds(0, 3 * (times - 1))]
        total = pltpu.make_async_remote_copy(
            src_ref=part, dst_ref=part, send_sem=row_send.at[k], recv_sem=row_recv.at[k],
            device_id=(after, s), device_id_type=MESH,
        )
        total.wait_recv()
        total.wait_send()
        one = coarse.at[pl.ds(0, 3)]
        pltpu.make_async_copy(one, one, local_sem.at[3 + k]).wait()


def place_outputs(arrived, settled, coarse, updated, rows_out, sem):
    half = updated.shape[2] // 2
    for i in range(arrived.shape[1]):
        lane = pl.ds(i * LANES, LANES)
        pltpu.make_async_copy(arrived.at[:, i], updated.at[0, :, :, lane], sem.at[0]).start()
        for side in range(2):
            pltpu.make_async_copy(
                settled.at[side, 0, :, i, pl.ds(HALO, half), :], updated.at[1, :, pl.ds(side * half, half), lane], sem.at[0]
            ).start()
    rows = pltpu.make_async_copy(coarse, rows_out, sem.at[1])
    rows.start()
    pltpu.make_async_copy(updated, updated, sem.at[0]).wait()
    rows.wait()


def solution(mesh):
    def on_device(c_points):
        intervals, fields, rows, columns = c_points.shape
        times = lax.axis_size("tm")
        blocks = columns // LANES
        full = rows + 2 * HALO
        wide = rows // 2 + 2 * HALO
        narrow = rows // 2 + 2 * FACTOR
        f32 = jnp.float32
        arrived, settled, coarse = pl.pallas_call(
            kernel,
            out_shape=(
                pltpu.VMEM((fields, blocks, rows, LANES), f32),
                pltpu.VMEM((2, 2, fields, blocks, wide, LANES), f32),
                pltpu.VMEM((2 * times * fields, blocks, LANES), f32),
            ),
            in_specs=[pl.BlockSpec(memory_space=pl.ANY)],
            out_specs=(pl.BlockSpec(memory_space=pltpu.VMEM),) * 3,
            scratch_shapes=[
                pltpu.VMEM((2, fields, blocks, full, LANES), f32),
                pltpu.VMEM((fields, blocks, HALO, LANES), f32),
                pltpu.VMEM((2, fields, wide // SUBLANES, SUBLANES, columns), f32),
                pltpu.VMEM((2, fields, narrow // SUBLANES, SUBLANES, columns), f32),
                pltpu.VMEM((2, fields, blocks, narrow, LANES), f32),
                pltpu.VMEM((2, 2, narrow * fields, blocks, LANES), f32),
                pltpu.SemaphoreType.DMA((5,)),
                pltpu.SemaphoreType.DMA((2, 2)),
                pltpu.SemaphoreType.DMA((2, 2)),
                pltpu.SemaphoreType.DMA((2,)),
                pltpu.SemaphoreType.DMA((2,)),
                pltpu.SemaphoreType.DMA,
                pltpu.SemaphoreType.DMA,
                pltpu.SemaphoreType.DMA((2,)),
                pltpu.SemaphoreType.DMA((2,)),
                pltpu.SemaphoreType.DMA,
                pltpu.SemaphoreType.DMA,
                pltpu.SemaphoreType.REGULAR((5,)),
            ],
            compiler_params=pltpu.CompilerParams(collective_id=0, has_side_effects=True),
        )(c_points)
        updated, coarse = pl.pallas_call(
            place_outputs,
            out_shape=(jax.ShapeDtypeStruct(c_points.shape, f32), jax.ShapeDtypeStruct(coarse.shape, f32)),
            in_specs=[pl.BlockSpec(memory_space=pl.ANY)] * 3,
            out_specs=(pl.BlockSpec(memory_space=pl.ANY),) * 2,
            scratch_shapes=[pltpu.SemaphoreType.DMA((2,))],
        )(*(pltpu.with_memory_space_constraint(x, pltpu.VMEM) for x in (arrived, settled, coarse)))
        return updated, coarse.reshape(2 * times, fields, 1, 1, columns)

    return jax.shard_map(
        on_device,
        mesh=mesh,
        in_specs=(P("tm", None, "space", None),),
        out_specs=(P("tm", None, "space", None), P(None, None, "space", "tm", None)),
        check_vma=False,
    )
```

```python
import jax
import jax.numpy as jnp
from jax import lax
from jax.experimental import pallas as pl
from jax.experimental.pallas import tpu as pltpu
from jax.sharding import PartitionSpec as P

FACTOR = 8
LANES = 128
HALO = 2 * FACTOR
SUBLANES = 8
UNROLL = 4
MOMENTUM_SCALE = 0.4
SQUARE_SCALE = 0.08
SCALE_BACK = [0.25 ** FACTOR, 0.25 ** FACTOR / MOMENTUM_SCALE, 0.25 ** FACTOR / MOMENTUM_SCALE]
RUN = 4
LINE = 4
CORES = 2
MESH = pl.DeviceIdType.MESH


def inverse(height):
    return 1.0 / height


def step_rows(src, dst, square):
    count = src.shape[1]
    columns = src.shape[3]

    def parts(b):
        h, p, q = src[0, b], src[1, b], src[2, b]
        r = inverse(h)
        u = p * r
        v = q * r
        mixed = u * q
        half = (h * square) * h
        east = u * p + half
        north = v * q + half
        from_east = (h - p, p - east, q - mixed)
        from_west = (h + p, p + east, q + mixed)
        from_north = (h - q, p - mixed, q - north)
        from_south = (h + q, p + mixed, q + north)
        across = [
            pltpu.roll(e, columns - 1, axis=1) + pltpu.roll(w, 1, axis=1)
            for e, w in zip(from_east, from_west)
        ]
        return across, from_north, from_south

    def put(b, across, north, south):
        for f in range(3):
            dst[f, b] = across[f] + (north[f] + south[f])

    first = parts(0)
    second = parts(1)
    older, old = first, second
    for b in range(2, count):
        new = parts(b)
        put(b - 1, old[0], new[1], older[2])
        older, old = old, new
    put(count - 1, old[0], [pltpu.roll(x, SUBLANES - 1, axis=0) for x in first[1]], older[2])
    put(0, first[0], second[1], [pltpu.roll(x, 1, axis=0) for x in old[2]])


def kernel(c_ref, arrived, settled, coarse, ext, relay, states, pushed, behind, stage,
           local_sem, halo_send, halo_recv, back_send, back_recv, on_send, on_recv, row_send, row_recv,
           relay_send, relay_recv, known_in):
    t = lax.axis_index("tm")
    s = lax.axis_index("space")
    times = lax.axis_size("tm")
    strips = lax.axis_size("space")
    rows, columns = c_ref.shape[2], c_ref.shape[3]
    blocks = columns // LANES
    half = rows // 2
    wide = half + 2 * HALO
    narrow = half + 2 * FACTOR
    low = lax.rem(s + strips - 1, strips)
    high = lax.rem(s + 1, strips)
    before = lax.rem(t + times - 1, times)
    after = lax.rem(t + 1, times)

    spot = lax.rem(s, RUN)
    ending = spot == RUN - 1
    starting = spot == 0
    outer = jnp.logical_or(ending, starting)
    inner = jnp.logical_not(outer)
    upward = (spot < 2).astype(jnp.int32)
    leads = jnp.logical_and(outer, s < strips // 2)
    follows = jnp.logical_and(outer, s >= strips // 2)
    distant = jnp.where(upward == 1, low, high)
    beyond = lax.rem(s + strips + 2 - 4 * upward, strips)

    plane = LINE * CORES
    place_in_line = lax.rem(t // CORES, LINE)
    partner = t + 1 - 2 * lax.rem(t, CORES)
    around = (lax.rem(t + plane, times), lax.rem(t + times - plane, times))
    fore = place_in_line < LINE - 1
    aft = place_in_line > 0
    along = 1 + jnp.logical_and(fore, aft).astype(jnp.int32)
    near_pair = t + CORES * (1 - 2 * lax.rem(place_in_line, 2))
    far_pair = t + 2 * CORES * (1 - 2 * (place_in_line // 2))

    def tell(semaphore, group, strip=s):
        pl.semaphore_signal(semaphore, inc=1, device_id=(group, strip), device_id_type=MESH)

    def tell_around(semaphore):
        for group in around:
            tell(semaphore, group)

        @pl.when(fore)
        def _():
            tell(semaphore, t + CORES)

        @pl.when(aft)
        def _():
            tell(semaphore, t - CORES)

    barrier = pltpu.get_barrier_semaphore()
    @pl.when(jnp.logical_not(jnp.logical_and(follows, upward == 1)))
    def _():
        tell(barrier, t, low)

    @pl.when(jnp.logical_not(jnp.logical_and(follows, upward == 0)))
    def _():
        tell(barrier, t, high)

    tell(barrier, partner)
    tell_around(barrier)

    lanes = [pl.ds(i * LANES, LANES) for i in range(blocks)]
    for k in range(2):
        for i in range(blocks):
            pltpu.make_async_copy(
                c_ref.at[k, :, :, lanes[i]], ext.at[k, :, i, pl.ds(HALO, rows), :], local_sem.at[k]
            ).start()
    opening = [
        pltpu.make_async_copy(c_ref.at[0, :, :, lanes[i]], arrived.at[:, i], local_sem.at[2]) for i in range(blocks)
    ]

    @pl.when(t == 0)
    def _():
        for copy in opening:
            copy.start()

    pl.semaphore_wait(barrier, 5 + along - leads.astype(jnp.int32))

    def halo_copy(side, k, source, target):
        return pltpu.make_async_remote_copy(
            src_ref=source, dst_ref=target, send_sem=halo_send.at[side, k], recv_sem=halo_recv.at[side, k],
            device_id=(t, low if side else high), device_id_type=MESH,
        )

    def halo_start(side, k, source, place):
        for i in range(blocks):
            halo_copy(
                side, k,
                c_ref.at[k, :, pl.ds(source, HALO), lanes[i]],
                ext.at[k, :, i, pl.ds(place, HALO), :],
            ).start()

    def side_start(side, k):
        halo_start(side, k, 0 if side else rows - HALO, HALO + rows if side else 0)

    def far_start():
        relay_start()
        for side in range(2):

            @pl.when(upward == side)
            def _():
                side_start(side, 0)

    def relay_start():
        source = pl.multiple_of((1 - upward) * (rows - HALO), SUBLANES)
        hop = jnp.where(upward == 1, high, low)
        for i in range(blocks):
            pltpu.make_async_remote_copy(
                src_ref=c_ref.at[1, :, pl.ds(source, HALO), lanes[i]], dst_ref=relay.at[:, i],
                send_sem=halo_send.at[upward, 1], recv_sem=relay_recv,
                device_id=(t, hop), device_id_type=MESH,
            ).start()

    @pl.when(follows)
    def _():
        tell(known_in.at[4], t, distant)
        far_start()

    for k in range(2):
        for side in range(2):

            @pl.when(jnp.logical_or(inner, upward != side))
            def _():
                side_start(side, k)

    def relay_copy():
        place = pl.multiple_of(upward * (HALO + rows), SUBLANES)
        return pltpu.make_async_remote_copy(
            src_ref=relay, dst_ref=ext.at[1, :, :, pl.ds(place, HALO), :],
            send_sem=relay_send, recv_sem=halo_recv.at[upward, 1],
            device_id=(t, beyond), device_id_type=MESH,
        )

    tell_around(known_in.at[0])
    pl.semaphore_wait(known_in.at[0], 2 + along)
    for stage_index, group in ((1, near_pair), (2, far_pair), (3, partner)):
        tell(known_in.at[stage_index], group)
        pl.semaphore_wait(known_in.at[stage_index], 1)

    def forward():
        pltpu.make_async_remote_copy(
            src_ref=relay, dst_ref=relay, send_sem=relay_send, recv_sem=relay_recv,
            device_id=(t, high), device_id_type=MESH,
        ).wait_recv()
        relay_copy().start()

    @pl.when(jnp.logical_and(inner, s >= strips // 2))
    def _():
        forward()

    def halo_bytes(side, k):
        part = ext.at[k, :, :, pl.ds(0, HALO), :]
        return pltpu.make_async_remote_copy(
            src_ref=part, dst_ref=part, send_sem=halo_send.at[side, k], recv_sem=halo_recv.at[side, k],
            device_id=(t, high), device_id_type=MESH,
        )

    def propagate(load, count, buffers):
        a = buffers.at[0, :, pl.ds(0, count)]
        b = buffers.at[1, :, pl.ds(0, count)]
        for f in range(3):
            for r in range(count):
                for i in range(blocks):
                    value = load(f, i, r, count)
                    a[f, r, :, i * LANES:(i + 1) * LANES] = value if f == 0 else value * MOMENTUM_SCALE

        def group(_, square):
            for source, target in ((a, b), (b, a)) * (UNROLL // 2):
                step_rows(source, target, square)
                square = square * 0.25
            return square

        lax.fori_loop(0, FACTOR // UNROLL, group, SQUARE_SCALE)
        return lambda f, i, r: a[f, r, :, i * LANES:(i + 1) * LANES] * SCALE_BACK[f]

    center = pl.ds(HALO, half)
    wrapped = t == times - 1

    def back_copy(w):
        return pltpu.make_async_remote_copy(
            src_ref=settled.at[w, 0, :, :, center, :], dst_ref=behind.at[w, :, :, pl.ds(FACTOR, half), :],
            send_sem=back_send.at[w], recv_sem=back_recv.at[w], device_id=(before, s), device_id_type=MESH,
        )

    def on_copy(w, offset):
        return pltpu.make_async_remote_copy(
            src_ref=settled.at[w, 1, :, :, center, :], dst_ref=arrived.at[:, :, pl.ds(offset, half), :],
            send_sem=on_send, recv_sem=on_recv, device_id=(after, s), device_id_type=MESH,
        )

    def send_rows(w, k, offset):
        place = coarse.at[pl.ds(lax.rem(2 * t + 1 + k, 2 * times) * 3, 3)]

        def row_copy(row):
            return pltpu.make_async_remote_copy(
                src_ref=stage.at[w, k, pl.ds((FACTOR + row) * 3, 3)], dst_ref=place,
                send_sem=row_send.at[k], recv_sem=row_recv.at[k],
                device_id=(offset + row, s), device_id_type=MESH,
            )

        @pl.loop(1, half)
        def _(d):
            row_copy(lax.rem(t + d, half)).start()

        last = lax.rem(t, half)

        @pl.when(offset + last != t)
        def _():
            row_copy(last).start()

        @pl.when(offset + last == t)
        def _():
            pltpu.make_async_copy(stage.at[w, k, pl.ds((FACTOR + last) * 3, 3)], place, local_sem.at[3 + k]).start()

    @pl.when(leads)
    def _():
        pl.semaphore_wait(known_in.at[4], 1)
        far_start()

    @pl.loop(0, 2)
    def _(w):
        side = lax.rem(w + upward, 2)
        offset = pl.multiple_of(side * half, SUBLANES)

        def advance(k):
            @pl.when(w == 0)
            def _():
                part = ext.at[k, :, :, pl.ds(HALO, rows), :]
                pltpu.make_async_copy(part, part, local_sem.at[k]).wait()

            halo_bytes(side, k).wait_recv()
            result = propagate(
                lambda f, i, r, count: ext[k, f, i, pl.ds(offset + r, SUBLANES, stride=count), :],
                wide // SUBLANES, states,
            )
            for f in range(3):
                for r in range(wide // SUBLANES):
                    for i in range(blocks):
                        settled[side, k, f, i, pl.ds(r, SUBLANES, stride=wide // SUBLANES), :] = result(f, i, r)

        def push(k, buffers):
            return propagate(
                lambda f, i, r, count: settled[side, k, f, i, pl.ds(FACTOR + r, SUBLANES, stride=count), :],
                narrow // SUBLANES, buffers,
            )

        def residual(k, result):
            count = narrow // SUBLANES
            for f in range(3):
                for r in range(count):
                    for i in range(blocks):
                        value = result(f, i, r)
                        if k == 0:
                            known = settled[side, 1, f, i, pl.ds(FACTOR + r, SUBLANES, stride=count), :]
                        else:
                            known = behind[side, f, i, pl.ds(r, SUBLANES, stride=count), :]
                            value = jnp.where(wrapped, known, value)
                        stage[side, k, pl.ds(r * 3 + f, SUBLANES, stride=3 * count), i, :] = value - known

        advance(0)

        back_copy(side).start()
        first = push(0, pushed)
        advance(1)

        @pl.when(t < times - 1)
        def _():
            on_copy(side, offset).start()

        residual(0, first)
        send_rows(side, 0, offset)
        @pl.when(jnp.logical_and(w == 0, jnp.logical_and(inner, s < strips // 2)))
        def _():
            forward()

        second = push(1, states)
        back_copy(side).wait_recv()
        residual(1, second)
        send_rows(side, 1, offset)

    for k in range(2):
        for side in range(2):
            halo_bytes(side, k).wait_send()
    for w in range(2):
        back_copy(w).wait_send()

    @pl.when(inner)
    def _():
        relay_copy().wait_send()

    whole = pltpu.make_async_remote_copy(
        src_ref=arrived, dst_ref=arrived, send_sem=on_send, recv_sem=on_recv,
        device_id=(after, s), device_id_type=MESH,
    )

    @pl.when(t == 0)
    def _():
        pltpu.make_async_copy(arrived, arrived, local_sem.at[2]).wait()

    @pl.when(t > 0)
    def _():
        whole.wait_recv()

    @pl.when(t < times - 1)
    def _():
        whole.wait_send()

    for k in range(2):
        part = coarse.at[pl.ds(0, 3 * (times - 1))]
        total = pltpu.make_async_remote_copy(
            src_ref=part, dst_ref=part, send_sem=row_send.at[k], recv_sem=row_recv.at[k],
            device_id=(after, s), device_id_type=MESH,
        )
        total.wait_recv()
        total.wait_send()
        one = coarse.at[pl.ds(0, 3)]
        pltpu.make_async_copy(one, one, local_sem.at[3 + k]).wait()


def place_outputs(arrived, settled, coarse, updated, rows_out, sem):
    half = updated.shape[2] // 2
    for i in range(arrived.shape[1]):
        lane = pl.ds(i * LANES, LANES)
        pltpu.make_async_copy(arrived.at[:, i], updated.at[0, :, :, lane], sem.at[0]).start()
        for side in range(2):
            pltpu.make_async_copy(
                settled.at[side, 0, :, i, pl.ds(HALO, half), :], updated.at[1, :, pl.ds(side * half, half), lane], sem.at[0]
            ).start()
    rows = pltpu.make_async_copy(coarse, rows_out, sem.at[1])
    rows.start()
    pltpu.make_async_copy(updated, updated, sem.at[0]).wait()
    rows.wait()


def solution(mesh):
    def on_device(c_points):
        intervals, fields, rows, columns = c_points.shape
        times = lax.axis_size("tm")
        blocks = columns // LANES
        full = rows + 2 * HALO
        wide = rows // 2 + 2 * HALO
        narrow = rows // 2 + 2 * FACTOR
        f32 = jnp.float32
        arrived, settled, coarse = pl.pallas_call(
            kernel,
            out_shape=(
                pltpu.VMEM((fields, blocks, rows, LANES), f32),
                pltpu.VMEM((2, 2, fields, blocks, wide, LANES), f32),
                pltpu.VMEM((2 * times * fields, blocks, LANES), f32),
            ),
            in_specs=[pl.BlockSpec(memory_space=pl.ANY)],
            out_specs=(pl.BlockSpec(memory_space=pltpu.VMEM),) * 3,
            scratch_shapes=[
                pltpu.VMEM((2, fields, blocks, full, LANES), f32),
                pltpu.VMEM((fields, blocks, HALO, LANES), f32),
                pltpu.VMEM((2, fields, wide // SUBLANES, SUBLANES, columns), f32),
                pltpu.VMEM((2, fields, narrow // SUBLANES, SUBLANES, columns), f32),
                pltpu.VMEM((2, fields, blocks, narrow, LANES), f32),
                pltpu.VMEM((2, 2, narrow * fields, blocks, LANES), f32),
                pltpu.SemaphoreType.DMA((5,)),
                pltpu.SemaphoreType.DMA((2, 2)),
                pltpu.SemaphoreType.DMA((2, 2)),
                pltpu.SemaphoreType.DMA((2,)),
                pltpu.SemaphoreType.DMA((2,)),
                pltpu.SemaphoreType.DMA,
                pltpu.SemaphoreType.DMA,
                pltpu.SemaphoreType.DMA((2,)),
                pltpu.SemaphoreType.DMA((2,)),
                pltpu.SemaphoreType.DMA,
                pltpu.SemaphoreType.DMA,
                pltpu.SemaphoreType.REGULAR((5,)),
            ],
            compiler_params=pltpu.CompilerParams(collective_id=0, has_side_effects=True),
        )(c_points)
        updated, coarse = pl.pallas_call(
            place_outputs,
            out_shape=(jax.ShapeDtypeStruct(c_points.shape, f32), jax.ShapeDtypeStruct(coarse.shape, f32)),
            in_specs=[pl.BlockSpec(memory_space=pl.ANY)] * 3,
            out_specs=(pl.BlockSpec(memory_space=pl.ANY),) * 2,
            scratch_shapes=[pltpu.SemaphoreType.DMA((2,))],
        )(*(pltpu.with_memory_space_constraint(x, pltpu.VMEM) for x in (arrived, settled, coarse)))
        return updated, coarse.reshape(2 * times, fields, 1, 1, columns)

    return jax.shard_map(
        on_device,
        mesh=mesh,
        in_specs=(P("tm", None, "space", None),),
        out_specs=(P("tm", None, "space", None), P(None, None, "space", "tm", None)),
        check_vma=False,
    )
```

```python
import jax
import jax.numpy as jnp
from jax import lax
from jax.experimental import pallas as pl
from jax.experimental.pallas import tpu as pltpu
from jax.sharding import PartitionSpec as P

FACTOR = 8
LANES = 128
HALO = 2 * FACTOR
SUBLANES = 8
UNROLL = 4
MOMENTUM_SCALE = 0.4
SQUARE_SCALE = 0.08
SCALE_BACK = [0.25 ** FACTOR, 0.25 ** FACTOR / MOMENTUM_SCALE, 0.25 ** FACTOR / MOMENTUM_SCALE]
RUN = 4
LINE = 4
CORES = 2
MESH = pl.DeviceIdType.MESH


def inverse(height):
    return 1.0 / height


def step_rows(src, dst, square):
    count = src.shape[1]
    columns = src.shape[3]

    def parts(b):
        h, p, q = src[0, b], src[1, b], src[2, b]
        r = inverse(h)
        u = p * r
        v = q * r
        mixed = u * q
        half = (h * square) * h
        east = u * p + half
        north = v * q + half
        from_east = (h - p, p - east, q - mixed)
        from_west = (h + p, p + east, q + mixed)
        from_north = (h - q, p - mixed, q - north)
        from_south = (h + q, p + mixed, q + north)
        across = [
            pltpu.roll(e, columns - 1, axis=1) + pltpu.roll(w, 1, axis=1)
            for e, w in zip(from_east, from_west)
        ]
        return across, from_north, from_south

    def put(b, across, north, south):
        for f in range(3):
            dst[f, b] = across[f] + (north[f] + south[f])

    first = parts(0)
    second = parts(1)
    older, old = first, second
    for b in range(2, count):
        new = parts(b)
        put(b - 1, old[0], new[1], older[2])
        older, old = old, new
    put(count - 1, old[0], [pltpu.roll(x, SUBLANES - 1, axis=0) for x in first[1]], older[2])
    put(0, first[0], second[1], [pltpu.roll(x, 1, axis=0) for x in old[2]])


def kernel(c_ref, arrived, settled, coarse, ext, relay, states, pushed, behind, stage,
           local_sem, halo_send, halo_recv, back_send, back_recv, on_send, on_recv, row_send, row_recv,
           relay_send, relay_recv, known_in):
    t = lax.axis_index("tm")
    s = lax.axis_index("space")
    times = lax.axis_size("tm")
    strips = lax.axis_size("space")
    rows, columns = c_ref.shape[2], c_ref.shape[3]
    blocks = columns // LANES
    half = rows // 2
    wide = half + 2 * HALO
    narrow = half + 2 * FACTOR
    low = lax.rem(s + strips - 1, strips)
    high = lax.rem(s + 1, strips)
    before = lax.rem(t + times - 1, times)
    after = lax.rem(t + 1, times)

    spot = lax.rem(s, RUN)
    ending = spot == RUN - 1
    starting = spot == 0
    outer = jnp.logical_or(ending, starting)
    inner = jnp.logical_not(outer)
    upward = (spot < 2).astype(jnp.int32)
    leads = jnp.logical_and(outer, s < strips // 2)
    follows = jnp.logical_and(outer, s >= strips // 2)
    distant = jnp.where(upward == 1, low, high)
    beyond = lax.rem(s + strips + 2 - 4 * upward, strips)

    plane = LINE * CORES
    place_in_line = lax.rem(t // CORES, LINE)
    partner = t + 1 - 2 * lax.rem(t, CORES)
    around = (lax.rem(t + plane, times), lax.rem(t + times - plane, times))
    fore = place_in_line < LINE - 1
    aft = place_in_line > 0
    along = 1 + jnp.logical_and(fore, aft).astype(jnp.int32)
    near_pair = t + CORES * (1 - 2 * lax.rem(place_in_line, 2))
    far_pair = t + 2 * CORES * (1 - 2 * (place_in_line // 2))

    def tell(semaphore, group, strip=s):
        pl.semaphore_signal(semaphore, inc=1, device_id=(group, strip), device_id_type=MESH)

    def tell_around(semaphore):
        for group in around:
            tell(semaphore, group)

        @pl.when(fore)
        def _():
            tell(semaphore, t + CORES)

        @pl.when(aft)
        def _():
            tell(semaphore, t - CORES)

    barrier = pltpu.get_barrier_semaphore()
    @pl.when(jnp.logical_not(jnp.logical_and(follows, upward == 1)))
    def _():
        tell(barrier, t, low)

    @pl.when(jnp.logical_not(jnp.logical_and(follows, upward == 0)))
    def _():
        tell(barrier, t, high)

    tell(barrier, partner)
    tell_around(barrier)

    lanes = [pl.ds(i * LANES, LANES) for i in range(blocks)]
    for k in range(2):
        for i in range(blocks):
            pltpu.make_async_copy(
                c_ref.at[k, :, :, lanes[i]], ext.at[k, :, i, pl.ds(HALO, rows), :], local_sem.at[k]
            ).start()
    opening = [
        pltpu.make_async_copy(c_ref.at[0, :, :, lanes[i]], arrived.at[:, i], local_sem.at[2]) for i in range(blocks)
    ]

    @pl.when(t == 0)
    def _():
        for copy in opening:
            copy.start()

    pl.semaphore_wait(barrier, 5 + along - leads.astype(jnp.int32))

    def halo_copy(side, k, source, target):
        return pltpu.make_async_remote_copy(
            src_ref=source, dst_ref=target, send_sem=halo_send.at[side, k], recv_sem=halo_recv.at[side, k],
            device_id=(t, low if side else high), device_id_type=MESH,
        )

    def halo_start(side, k, source, place):
        for i in range(blocks):
            halo_copy(
                side, k,
                c_ref.at[k, :, pl.ds(source, HALO), lanes[i]],
                ext.at[k, :, i, pl.ds(place, HALO), :],
            ).start()

    def side_start(side, k):
        halo_start(side, k, 0 if side else rows - HALO, HALO + rows if side else 0)

    def far_start():
        relay_start()
        for side in range(2):

            @pl.when(upward == side)
            def _():
                side_start(side, 0)

    def relay_start():
        source = pl.multiple_of((1 - upward) * (rows - HALO), SUBLANES)
        hop = jnp.where(upward == 1, high, low)
        for i in range(blocks):
            pltpu.make_async_remote_copy(
                src_ref=c_ref.at[1, :, pl.ds(source, HALO), lanes[i]], dst_ref=relay.at[:, i],
                send_sem=halo_send.at[upward, 1], recv_sem=relay_recv,
                device_id=(t, hop), device_id_type=MESH,
            ).start()

    @pl.when(follows)
    def _():
        tell(known_in.at[4], t, distant)
        far_start()

    for k in range(2):
        for side in range(2):

            @pl.when(jnp.logical_or(inner, upward != side))
            def _():
                side_start(side, k)

    def relay_copy():
        place = pl.multiple_of(upward * (HALO + rows), SUBLANES)
        return pltpu.make_async_remote_copy(
            src_ref=relay, dst_ref=ext.at[1, :, :, pl.ds(place, HALO), :],
            send_sem=relay_send, recv_sem=halo_recv.at[upward, 1],
            device_id=(t, beyond), device_id_type=MESH,
        )

    tell_around(known_in.at[0])
    pl.semaphore_wait(known_in.at[0], 2 + along)
    for stage_index, group in ((1, near_pair), (2, far_pair), (3, partner)):
        tell(known_in.at[stage_index], group)
        pl.semaphore_wait(known_in.at[stage_index], 1)

    def forward():
        pltpu.make_async_remote_copy(
            src_ref=relay, dst_ref=relay, send_sem=relay_send, recv_sem=relay_recv,
            device_id=(t, high), device_id_type=MESH,
        ).wait_recv()
        relay_copy().start()

    @pl.when(jnp.logical_and(inner, s >= strips // 2))
    def _():
        forward()

    def halo_bytes(side, k):
        part = ext.at[k, :, :, pl.ds(0, HALO), :]
        return pltpu.make_async_remote_copy(
            src_ref=part, dst_ref=part, send_sem=halo_send.at[side, k], recv_sem=halo_recv.at[side, k],
            device_id=(t, high), device_id_type=MESH,
        )

    def propagate(load, count, buffers):
        a = buffers.at[0, :, pl.ds(0, count)]
        b = buffers.at[1, :, pl.ds(0, count)]
        for f in range(3):
            for r in range(count):
                for i in range(blocks):
                    value = load(f, i, r, count)
                    a[f, r, :, i * LANES:(i + 1) * LANES] = value if f == 0 else value * MOMENTUM_SCALE

        def group(_, square):
            for source, target in ((a, b), (b, a)) * (UNROLL // 2):
                step_rows(source, target, square)
                square = square * 0.25
            return square

        lax.fori_loop(0, FACTOR // UNROLL, group, SQUARE_SCALE)
        return lambda f, i, r: a[f, r, :, i * LANES:(i + 1) * LANES] * SCALE_BACK[f]

    center = pl.ds(HALO, half)
    wrapped = t == times - 1

    def back_copy(w):
        return pltpu.make_async_remote_copy(
            src_ref=settled.at[w, 0, :, :, center, :], dst_ref=behind.at[w, :, :, pl.ds(FACTOR, half), :],
            send_sem=back_send.at[w], recv_sem=back_recv.at[w], device_id=(before, s), device_id_type=MESH,
        )

    def on_copy(w, offset):
        return pltpu.make_async_remote_copy(
            src_ref=settled.at[w, 1, :, :, center, :], dst_ref=arrived.at[:, :, pl.ds(offset, half), :],
            send_sem=on_send, recv_sem=on_recv, device_id=(after, s), device_id_type=MESH,
        )

    def send_rows(w, k, offset):
        place = coarse.at[pl.ds(lax.rem(2 * t + 1 + k, 2 * times) * 3, 3)]

        def row_copy(row):
            return pltpu.make_async_remote_copy(
                src_ref=stage.at[w, k, pl.ds((FACTOR + row) * 3, 3)], dst_ref=place,
                send_sem=row_send.at[k], recv_sem=row_recv.at[k],
                device_id=(offset + row, s), device_id_type=MESH,
            )

        @pl.loop(1, half)
        def _(d):
            row_copy(lax.rem(t + d, half)).start()

        last = lax.rem(t, half)

        @pl.when(offset + last != t)
        def _():
            row_copy(last).start()

        @pl.when(offset + last == t)
        def _():
            pltpu.make_async_copy(stage.at[w, k, pl.ds((FACTOR + last) * 3, 3)], place, local_sem.at[3 + k]).start()

    @pl.when(leads)
    def _():
        pl.semaphore_wait(known_in.at[4], 1)
        far_start()

    @pl.loop(0, 2)
    def _(w):
        side = lax.rem(w + upward, 2)
        offset = pl.multiple_of(side * half, SUBLANES)

        def advance(k):
            @pl.when(w == 0)
            def _():
                part = ext.at[k, :, :, pl.ds(HALO, rows), :]
                pltpu.make_async_copy(part, part, local_sem.at[k]).wait()

            halo_bytes(side, k).wait_recv()
            result = propagate(
                lambda f, i, r, count: ext[k, f, i, pl.ds(offset + r, SUBLANES, stride=count), :],
                wide // SUBLANES, states,
            )
            for f in range(3):
                for r in range(wide // SUBLANES):
                    for i in range(blocks):
                        settled[side, k, f, i, pl.ds(r, SUBLANES, stride=wide // SUBLANES), :] = result(f, i, r)

        def push(k, buffers):
            return propagate(
                lambda f, i, r, count: settled[side, k, f, i, pl.ds(FACTOR + r, SUBLANES, stride=count), :],
                narrow // SUBLANES, buffers,
            )

        def residual(k, result):
            count = narrow // SUBLANES
            for f in range(3):
                for r in range(count):
                    for i in range(blocks):
                        value = result(f, i, r)
                        if k == 0:
                            known = settled[side, 1, f, i, pl.ds(FACTOR + r, SUBLANES, stride=count), :]
                        else:
                            known = behind[side, f, i, pl.ds(r, SUBLANES, stride=count), :]
                            value = jnp.where(wrapped, known, value)
                        stage[side, k, pl.ds(r * 3 + f, SUBLANES, stride=3 * count), i, :] = value - known

        advance(0)

        back_copy(side).start()
        first = push(0, pushed)
        advance(1)

        residual(0, first)
        send_rows(side, 0, offset)
        @pl.when(jnp.logical_and(w == 0, jnp.logical_and(inner, s < strips // 2)))
        def _():
            forward()

        second = push(1, states)
        back_copy(side).wait_recv()
        residual(1, second)
        send_rows(side, 1, offset)

        @pl.when(t < times - 1)
        def _():
            on_copy(side, offset).start()


    for k in range(2):
        for side in range(2):
            halo_bytes(side, k).wait_send()
    for w in range(2):
        back_copy(w).wait_send()

    @pl.when(inner)
    def _():
        relay_copy().wait_send()

    whole = pltpu.make_async_remote_copy(
        src_ref=arrived, dst_ref=arrived, send_sem=on_send, recv_sem=on_recv,
        device_id=(after, s), device_id_type=MESH,
    )

    @pl.when(t == 0)
    def _():
        pltpu.make_async_copy(arrived, arrived, local_sem.at[2]).wait()

    @pl.when(t > 0)
    def _():
        whole.wait_recv()

    @pl.when(t < times - 1)
    def _():
        whole.wait_send()

    for k in range(2):
        part = coarse.at[pl.ds(0, 3 * (times - 1))]
        total = pltpu.make_async_remote_copy(
            src_ref=part, dst_ref=part, send_sem=row_send.at[k], recv_sem=row_recv.at[k],
            device_id=(after, s), device_id_type=MESH,
        )
        total.wait_recv()
        total.wait_send()
        one = coarse.at[pl.ds(0, 3)]
        pltpu.make_async_copy(one, one, local_sem.at[3 + k]).wait()


def place_outputs(arrived, settled, coarse, updated, rows_out, sem):
    half = updated.shape[2] // 2
    for i in range(arrived.shape[1]):
        lane = pl.ds(i * LANES, LANES)
        pltpu.make_async_copy(arrived.at[:, i], updated.at[0, :, :, lane], sem.at[0]).start()
        for side in range(2):
            pltpu.make_async_copy(
                settled.at[side, 0, :, i, pl.ds(HALO, half), :], updated.at[1, :, pl.ds(side * half, half), lane], sem.at[0]
            ).start()
    rows = pltpu.make_async_copy(coarse, rows_out, sem.at[1])
    rows.start()
    pltpu.make_async_copy(updated, updated, sem.at[0]).wait()
    rows.wait()


def solution(mesh):
    def on_device(c_points):
        intervals, fields, rows, columns = c_points.shape
        times = lax.axis_size("tm")
        blocks = columns // LANES
        full = rows + 2 * HALO
        wide = rows // 2 + 2 * HALO
        narrow = rows // 2 + 2 * FACTOR
        f32 = jnp.float32
        arrived, settled, coarse = pl.pallas_call(
            kernel,
            out_shape=(
                pltpu.VMEM((fields, blocks, rows, LANES), f32),
                pltpu.VMEM((2, 2, fields, blocks, wide, LANES), f32),
                pltpu.VMEM((2 * times * fields, blocks, LANES), f32),
            ),
            in_specs=[pl.BlockSpec(memory_space=pl.ANY)],
            out_specs=(pl.BlockSpec(memory_space=pltpu.VMEM),) * 3,
            scratch_shapes=[
                pltpu.VMEM((2, fields, blocks, full, LANES), f32),
                pltpu.VMEM((fields, blocks, HALO, LANES), f32),
                pltpu.VMEM((2, fields, wide // SUBLANES, SUBLANES, columns), f32),
                pltpu.VMEM((2, fields, narrow // SUBLANES, SUBLANES, columns), f32),
                pltpu.VMEM((2, fields, blocks, narrow, LANES), f32),
                pltpu.VMEM((2, 2, narrow * fields, blocks, LANES), f32),
                pltpu.SemaphoreType.DMA((5,)),
                pltpu.SemaphoreType.DMA((2, 2)),
                pltpu.SemaphoreType.DMA((2, 2)),
                pltpu.SemaphoreType.DMA((2,)),
                pltpu.SemaphoreType.DMA((2,)),
                pltpu.SemaphoreType.DMA,
                pltpu.SemaphoreType.DMA,
                pltpu.SemaphoreType.DMA((2,)),
                pltpu.SemaphoreType.DMA((2,)),
                pltpu.SemaphoreType.DMA,
                pltpu.SemaphoreType.DMA,
                pltpu.SemaphoreType.REGULAR((5,)),
            ],
            compiler_params=pltpu.CompilerParams(collective_id=0, has_side_effects=True),
        )(c_points)
        updated, coarse = pl.pallas_call(
            place_outputs,
            out_shape=(jax.ShapeDtypeStruct(c_points.shape, f32), jax.ShapeDtypeStruct(coarse.shape, f32)),
            in_specs=[pl.BlockSpec(memory_space=pl.ANY)] * 3,
            out_specs=(pl.BlockSpec(memory_space=pl.ANY),) * 2,
            scratch_shapes=[pltpu.SemaphoreType.DMA((2,))],
        )(*(pltpu.with_memory_space_constraint(x, pltpu.VMEM) for x in (arrived, settled, coarse)))
        return updated, coarse.reshape(2 * times, fields, 1, 1, columns)

    return jax.shard_map(
        on_device,
        mesh=mesh,
        in_specs=(P("tm", None, "space", None),),
        out_specs=(P("tm", None, "space", None), P(None, None, "space", "tm", None)),
        check_vma=False,
    )
```

```python
import jax
import jax.numpy as jnp
from jax import lax
from jax.experimental import pallas as pl
from jax.experimental.pallas import tpu as pltpu
from jax.sharding import PartitionSpec as P

FACTOR = 8
LANES = 128
HALO = 2 * FACTOR
SUBLANES = 8
UNROLL = 4
MOMENTUM_SCALE = 0.4
SQUARE_SCALE = 0.08
SCALE_BACK = [0.25 ** FACTOR, 0.25 ** FACTOR / MOMENTUM_SCALE, 0.25 ** FACTOR / MOMENTUM_SCALE]
RUN = 4
LINE = 4
CORES = 2
MESH = pl.DeviceIdType.MESH


def inverse(height):
    return 1.0 / height


def step_rows(src, dst, square):
    count = src.shape[1]
    columns = src.shape[3]

    def parts(b):
        h, p, q = src[0, b], src[1, b], src[2, b]
        r = inverse(h)
        u = p * r
        v = q * r
        mixed = u * q
        half = (h * square) * h
        east = u * p + half
        north = v * q + half
        from_east = (h - p, p - east, q - mixed)
        from_west = (h + p, p + east, q + mixed)
        from_north = (h - q, p - mixed, q - north)
        from_south = (h + q, p + mixed, q + north)
        across = [
            pltpu.roll(e, columns - 1, axis=1) + pltpu.roll(w, 1, axis=1)
            for e, w in zip(from_east, from_west)
        ]
        return across, from_north, from_south

    def put(b, across, north, south):
        for f in range(3):
            dst[f, b] = across[f] + (north[f] + south[f])

    first = parts(0)
    second = parts(1)
    older, old = first, second
    for b in range(2, count):
        new = parts(b)
        put(b - 1, old[0], new[1], older[2])
        older, old = old, new
    put(count - 1, old[0], [pltpu.roll(x, SUBLANES - 1, axis=0) for x in first[1]], older[2])
    put(0, first[0], second[1], [pltpu.roll(x, 1, axis=0) for x in old[2]])


def kernel(c_ref, arrived, settled, coarse, ext, relay, states, pushed, behind, stage,
           local_sem, halo_send, halo_recv, back_send, back_recv, on_send, on_recv, row_send, row_recv,
           relay_send, relay_recv, known_in):
    t = lax.axis_index("tm")
    s = lax.axis_index("space")
    times = lax.axis_size("tm")
    strips = lax.axis_size("space")
    rows, columns = c_ref.shape[2], c_ref.shape[3]
    blocks = columns // LANES
    half = rows // 2
    wide = half + 2 * HALO
    narrow = half + 2 * FACTOR
    low = lax.rem(s + strips - 1, strips)
    high = lax.rem(s + 1, strips)
    before = lax.rem(t + times - 1, times)
    after = lax.rem(t + 1, times)

    spot = lax.rem(s, RUN)
    ending = spot == RUN - 1
    starting = spot == 0
    outer = jnp.logical_or(ending, starting)
    inner = jnp.logical_not(outer)
    upward = (spot < 2).astype(jnp.int32)
    leads = jnp.logical_and(outer, s < strips // 2)
    follows = jnp.logical_and(outer, s >= strips // 2)
    distant = jnp.where(upward == 1, low, high)
    beyond = lax.rem(s + strips + 2 - 4 * upward, strips)

    plane = LINE * CORES
    place_in_line = lax.rem(t // CORES, LINE)
    partner = t + 1 - 2 * lax.rem(t, CORES)
    around = (lax.rem(t + plane, times), lax.rem(t + times - plane, times))
    fore = place_in_line < LINE - 1
    aft = place_in_line > 0
    along = 1 + jnp.logical_and(fore, aft).astype(jnp.int32)
    near_pair = t + CORES * (1 - 2 * lax.rem(place_in_line, 2))
    far_pair = t + 2 * CORES * (1 - 2 * (place_in_line // 2))

    def tell(semaphore, group, strip=s):
        pl.semaphore_signal(semaphore, inc=1, device_id=(group, strip), device_id_type=MESH)

    def tell_around(semaphore):
        for group in around:
            tell(semaphore, group)

        @pl.when(fore)
        def _():
            tell(semaphore, t + CORES)

        @pl.when(aft)
        def _():
            tell(semaphore, t - CORES)

    barrier = pltpu.get_barrier_semaphore()
    @pl.when(jnp.logical_not(jnp.logical_and(follows, upward == 1)))
    def _():
        tell(barrier, t, low)

    @pl.when(jnp.logical_not(jnp.logical_and(follows, upward == 0)))
    def _():
        tell(barrier, t, high)

    tell(barrier, partner)
    tell_around(barrier)

    lanes = [pl.ds(i * LANES, LANES) for i in range(blocks)]
    for k in range(2):
        for i in range(blocks):
            pltpu.make_async_copy(
                c_ref.at[k, :, :, lanes[i]], ext.at[k, :, i, pl.ds(HALO, rows), :], local_sem.at[k]
            ).start()
    opening = [
        pltpu.make_async_copy(c_ref.at[0, :, :, lanes[i]], arrived.at[:, i], local_sem.at[2]) for i in range(blocks)
    ]

    @pl.when(t == 0)
    def _():
        for copy in opening:
            copy.start()

    pl.semaphore_wait(barrier, 5 + along - leads.astype(jnp.int32))

    def halo_copy(side, k, source, target):
        return pltpu.make_async_remote_copy(
            src_ref=source, dst_ref=target, send_sem=halo_send.at[side, k], recv_sem=halo_recv.at[side, k],
            device_id=(t, low if side else high), device_id_type=MESH,
        )

    def halo_start(side, k, source, place):
        for i in range(blocks):
            halo_copy(
                side, k,
                c_ref.at[k, :, pl.ds(source, HALO), lanes[i]],
                ext.at[k, :, i, pl.ds(place, HALO), :],
            ).start()

    def side_start(side, k):
        halo_start(side, k, 0 if side else rows - HALO, HALO + rows if side else 0)

    def far_start():
        relay_start()
        for side in range(2):

            @pl.when(upward == side)
            def _():
                side_start(side, 0)

    def relay_start():
        source = pl.multiple_of((1 - upward) * (rows - HALO), SUBLANES)
        hop = jnp.where(upward == 1, high, low)
        for i in range(blocks):
            pltpu.make_async_remote_copy(
                src_ref=c_ref.at[1, :, pl.ds(source, HALO), lanes[i]], dst_ref=relay.at[:, i],
                send_sem=halo_send.at[upward, 1], recv_sem=relay_recv,
                device_id=(t, hop), device_id_type=MESH,
            ).start()

    @pl.when(follows)
    def _():
        tell(known_in.at[4], t, distant)
        far_start()

    for k in range(2):
        for side in range(2):

            @pl.when(jnp.logical_or(inner, upward != side))
            def _():
                side_start(side, k)

    def relay_copy():
        place = pl.multiple_of(upward * (HALO + rows), SUBLANES)
        return pltpu.make_async_remote_copy(
            src_ref=relay, dst_ref=ext.at[1, :, :, pl.ds(place, HALO), :],
            send_sem=relay_send, recv_sem=halo_recv.at[upward, 1],
            device_id=(t, beyond), device_id_type=MESH,
        )

    tell_around(known_in.at[0])
    pl.semaphore_wait(known_in.at[0], 2 + along)
    for stage_index, group in ((1, near_pair), (2, far_pair), (3, partner)):
        tell(known_in.at[stage_index], group)
        pl.semaphore_wait(known_in.at[stage_index], 1)

    def forward():
        pltpu.make_async_remote_copy(
            src_ref=relay, dst_ref=relay, send_sem=relay_send, recv_sem=relay_recv,
            device_id=(t, high), device_id_type=MESH,
        ).wait_recv()
        relay_copy().start()

    @pl.when(jnp.logical_and(inner, s >= strips // 2))
    def _():
        forward()

    def halo_bytes(side, k):
        part = ext.at[k, :, :, pl.ds(0, HALO), :]
        return pltpu.make_async_remote_copy(
            src_ref=part, dst_ref=part, send_sem=halo_send.at[side, k], recv_sem=halo_recv.at[side, k],
            device_id=(t, high), device_id_type=MESH,
        )

    def propagate(load, count, buffers):
        a = buffers.at[0, :, pl.ds(0, count)]
        b = buffers.at[1, :, pl.ds(0, count)]
        for f in range(3):
            for r in range(count):
                for i in range(blocks):
                    value = load(f, i, r, count)
                    a[f, r, :, i * LANES:(i + 1) * LANES] = value if f == 0 else value * MOMENTUM_SCALE

        def group(_, square):
            for source, target in ((a, b), (b, a)) * (UNROLL // 2):
                step_rows(source, target, square)
                square = square * 0.25
            return square

        lax.fori_loop(0, FACTOR // UNROLL, group, SQUARE_SCALE)
        return lambda f, i, r: a[f, r, :, i * LANES:(i + 1) * LANES] * SCALE_BACK[f]

    center = pl.ds(HALO, half)
    wrapped = t == times - 1

    def back_copy(w):
        return pltpu.make_async_remote_copy(
            src_ref=settled.at[w, 0, :, :, center, :], dst_ref=behind.at[w, :, :, pl.ds(FACTOR, half), :],
            send_sem=back_send.at[w], recv_sem=back_recv.at[w], device_id=(before, s), device_id_type=MESH,
        )

    def on_copy(w, offset):
        return pltpu.make_async_remote_copy(
            src_ref=settled.at[w, 1, :, :, center, :], dst_ref=arrived.at[:, :, pl.ds(offset, half), :],
            send_sem=on_send, recv_sem=on_recv, device_id=(after, s), device_id_type=MESH,
        )

    def send_rows(w, k, offset):
        place = coarse.at[pl.ds(lax.rem(2 * t + 1 + k, 2 * times) * 3, 3)]

        def row_copy(row):
            return pltpu.make_async_remote_copy(
                src_ref=stage.at[w, k, pl.ds((FACTOR + row) * 3, 3)], dst_ref=place,
                send_sem=row_send.at[k], recv_sem=row_recv.at[k],
                device_id=(offset + row, s), device_id_type=MESH,
            )

        @pl.loop(1, half)
        def _(d):
            row_copy(lax.rem(t + d, half)).start()

        last = lax.rem(t, half)

        @pl.when(offset + last != t)
        def _():
            row_copy(last).start()

        @pl.when(offset + last == t)
        def _():
            pltpu.make_async_copy(stage.at[w, k, pl.ds((FACTOR + last) * 3, 3)], place, local_sem.at[3 + k]).start()

    @pl.when(leads)
    def _():
        pl.semaphore_wait(known_in.at[4], 1)
        far_start()

    @pl.loop(0, 2)
    def _(w):
        side = lax.rem(w + upward, 2)
        offset = pl.multiple_of(side * half, SUBLANES)

        def advance(k):
            @pl.when(w == 0)
            def _():
                part = ext.at[k, :, :, pl.ds(HALO, rows), :]
                pltpu.make_async_copy(part, part, local_sem.at[k]).wait()

            halo_bytes(side, k).wait_recv()
            result = propagate(
                lambda f, i, r, count: ext[k, f, i, pl.ds(offset + r, SUBLANES, stride=count), :],
                wide // SUBLANES, states,
            )
            for f in range(3):
                for r in range(wide // SUBLANES):
                    for i in range(blocks):
                        settled[side, k, f, i, pl.ds(r, SUBLANES, stride=wide // SUBLANES), :] = result(f, i, r)

        def push(k, buffers):
            return propagate(
                lambda f, i, r, count: settled[side, k, f, i, pl.ds(FACTOR + r, SUBLANES, stride=count), :],
                narrow // SUBLANES, buffers,
            )

        def residual(k, result):
            count = narrow // SUBLANES
            for f in range(3):
                for r in range(count):
                    for i in range(blocks):
                        value = result(f, i, r)
                        if k == 0:
                            known = settled[side, 1, f, i, pl.ds(FACTOR + r, SUBLANES, stride=count), :]
                        else:
                            known = behind[side, f, i, pl.ds(r, SUBLANES, stride=count), :]
                            value = jnp.where(wrapped, known, value)
                        stage[side, k, pl.ds(r * 3 + f, SUBLANES, stride=3 * count), i, :] = value - known

        advance(0)

        back_copy(side).start()
        first = push(0, pushed)
        advance(1)

        residual(0, first)
        send_rows(side, 0, offset)
        @pl.when(jnp.logical_and(w == 0, jnp.logical_and(inner, s < strips // 2)))
        def _():
            forward()

        second = push(1, states)
        back_copy(side).wait_recv()
        residual(1, second)
        send_rows(side, 1, offset)

        @pl.when(jnp.logical_and(t < times - 1, outer))
        def _():
            on_copy(side, offset).start()


    @pl.when(jnp.logical_and(t < times - 1, inner))
    def _():
        for side in range(2):
            on_copy(side, side * half).start()

    for k in range(2):
        for side in range(2):
            halo_bytes(side, k).wait_send()
    for w in range(2):
        back_copy(w).wait_send()

    @pl.when(inner)
    def _():
        relay_copy().wait_send()

    whole = pltpu.make_async_remote_copy(
        src_ref=arrived, dst_ref=arrived, send_sem=on_send, recv_sem=on_recv,
        device_id=(after, s), device_id_type=MESH,
    )

    @pl.when(t == 0)
    def _():
        pltpu.make_async_copy(arrived, arrived, local_sem.at[2]).wait()

    @pl.when(t > 0)
    def _():
        whole.wait_recv()

    @pl.when(t < times - 1)
    def _():
        whole.wait_send()

    for k in range(2):
        part = coarse.at[pl.ds(0, 3 * (times - 1))]
        total = pltpu.make_async_remote_copy(
            src_ref=part, dst_ref=part, send_sem=row_send.at[k], recv_sem=row_recv.at[k],
            device_id=(after, s), device_id_type=MESH,
        )
        total.wait_recv()
        total.wait_send()
        one = coarse.at[pl.ds(0, 3)]
        pltpu.make_async_copy(one, one, local_sem.at[3 + k]).wait()


def place_outputs(arrived, settled, coarse, updated, rows_out, sem):
    half = updated.shape[2] // 2
    for i in range(arrived.shape[1]):
        lane = pl.ds(i * LANES, LANES)
        pltpu.make_async_copy(arrived.at[:, i], updated.at[0, :, :, lane], sem.at[0]).start()
        for side in range(2):
            pltpu.make_async_copy(
                settled.at[side, 0, :, i, pl.ds(HALO, half), :], updated.at[1, :, pl.ds(side * half, half), lane], sem.at[0]
            ).start()
    rows = pltpu.make_async_copy(coarse, rows_out, sem.at[1])
    rows.start()
    pltpu.make_async_copy(updated, updated, sem.at[0]).wait()
    rows.wait()


def solution(mesh):
    def on_device(c_points):
        intervals, fields, rows, columns = c_points.shape
        times = lax.axis_size("tm")
        blocks = columns // LANES
        full = rows + 2 * HALO
        wide = rows // 2 + 2 * HALO
        narrow = rows // 2 + 2 * FACTOR
        f32 = jnp.float32
        arrived, settled, coarse = pl.pallas_call(
            kernel,
            out_shape=(
                pltpu.VMEM((fields, blocks, rows, LANES), f32),
                pltpu.VMEM((2, 2, fields, blocks, wide, LANES), f32),
                pltpu.VMEM((2 * times * fields, blocks, LANES), f32),
            ),
            in_specs=[pl.BlockSpec(memory_space=pl.ANY)],
            out_specs=(pl.BlockSpec(memory_space=pltpu.VMEM),) * 3,
            scratch_shapes=[
                pltpu.VMEM((2, fields, blocks, full, LANES), f32),
                pltpu.VMEM((fields, blocks, HALO, LANES), f32),
                pltpu.VMEM((2, fields, wide // SUBLANES, SUBLANES, columns), f32),
                pltpu.VMEM((2, fields, narrow // SUBLANES, SUBLANES, columns), f32),
                pltpu.VMEM((2, fields, blocks, narrow, LANES), f32),
                pltpu.VMEM((2, 2, narrow * fields, blocks, LANES), f32),
                pltpu.SemaphoreType.DMA((5,)),
                pltpu.SemaphoreType.DMA((2, 2)),
                pltpu.SemaphoreType.DMA((2, 2)),
                pltpu.SemaphoreType.DMA((2,)),
                pltpu.SemaphoreType.DMA((2,)),
                pltpu.SemaphoreType.DMA,
                pltpu.SemaphoreType.DMA,
                pltpu.SemaphoreType.DMA((2,)),
                pltpu.SemaphoreType.DMA((2,)),
                pltpu.SemaphoreType.DMA,
                pltpu.SemaphoreType.DMA,
                pltpu.SemaphoreType.REGULAR((5,)),
            ],
            compiler_params=pltpu.CompilerParams(collective_id=0, has_side_effects=True),
        )(c_points)
        updated, coarse = pl.pallas_call(
            place_outputs,
            out_shape=(jax.ShapeDtypeStruct(c_points.shape, f32), jax.ShapeDtypeStruct(coarse.shape, f32)),
            in_specs=[pl.BlockSpec(memory_space=pl.ANY)] * 3,
            out_specs=(pl.BlockSpec(memory_space=pl.ANY),) * 2,
            scratch_shapes=[pltpu.SemaphoreType.DMA((2,))],
        )(*(pltpu.with_memory_space_constraint(x, pltpu.VMEM) for x in (arrived, settled, coarse)))
        return updated, coarse.reshape(2 * times, fields, 1, 1, columns)

    return jax.shard_map(
        on_device,
        mesh=mesh,
        in_specs=(P("tm", None, "space", None),),
        out_specs=(P("tm", None, "space", None), P(None, None, "space", "tm", None)),
        check_vma=False,
    )
```

```python
import jax
import jax.numpy as jnp
from jax import lax
from jax.experimental import pallas as pl
from jax.experimental.pallas import tpu as pltpu
from jax.sharding import PartitionSpec as P

FACTOR = 8
LANES = 128
HALO = 2 * FACTOR
SUBLANES = 8
UNROLL = 4
MOMENTUM_SCALE = 0.4
SQUARE_SCALE = 0.08
SCALE_BACK = [0.25 ** FACTOR, 0.25 ** FACTOR / MOMENTUM_SCALE, 0.25 ** FACTOR / MOMENTUM_SCALE]
RUN = 4
LINE = 4
CORES = 2
MESH = pl.DeviceIdType.MESH


def inverse(height):
    return 1.0 / height


def step_rows(src, dst, square):
    count = src.shape[1]
    columns = src.shape[3]

    def parts(b):
        h, p, q = src[0, b], src[1, b], src[2, b]
        r = inverse(h)
        u = p * r
        v = q * r
        mixed = u * q
        half = (h * square) * h
        east = u * p + half
        north = v * q + half
        from_east = (h - p, p - east, q - mixed)
        from_west = (h + p, p + east, q + mixed)
        from_north = (h - q, p - mixed, q - north)
        from_south = (h + q, p + mixed, q + north)
        across = [
            pltpu.roll(e, columns - 1, axis=1) + pltpu.roll(w, 1, axis=1)
            for e, w in zip(from_east, from_west)
        ]
        return across, from_north, from_south

    def put(b, across, north, south):
        for f in range(3):
            dst[f, b] = across[f] + (north[f] + south[f])

    first = parts(0)
    second = parts(1)
    older, old = first, second
    for b in range(2, count):
        new = parts(b)
        put(b - 1, old[0], new[1], older[2])
        older, old = old, new
    put(count - 1, old[0], [pltpu.roll(x, SUBLANES - 1, axis=0) for x in first[1]], older[2])
    put(0, first[0], second[1], [pltpu.roll(x, 1, axis=0) for x in old[2]])


def kernel(c_ref, arrived, settled, coarse, ext, relay, states, pushed, behind, stage,
           local_sem, halo_send, halo_recv, back_send, back_recv, on_send, on_recv, row_send, row_recv,
           relay_send, relay_recv, known_in):
    t = lax.axis_index("tm")
    s = lax.axis_index("space")
    times = lax.axis_size("tm")
    strips = lax.axis_size("space")
    rows, columns = c_ref.shape[2], c_ref.shape[3]
    blocks = columns // LANES
    half = rows // 2
    wide = half + 2 * HALO
    narrow = half + 2 * FACTOR
    low = lax.rem(s + strips - 1, strips)
    high = lax.rem(s + 1, strips)
    before = lax.rem(t + times - 1, times)
    after = lax.rem(t + 1, times)

    spot = lax.rem(s, RUN)
    ending = spot == RUN - 1
    starting = spot == 0
    outer = jnp.logical_or(ending, starting)
    inner = jnp.logical_not(outer)
    upward = (spot < 2).astype(jnp.int32)
    leads = jnp.logical_and(outer, s < strips // 2)
    follows = jnp.logical_and(outer, s >= strips // 2)
    distant = jnp.where(upward == 1, low, high)
    beyond = lax.rem(s + strips + 2 - 4 * upward, strips)

    plane = LINE * CORES
    place_in_line = lax.rem(t // CORES, LINE)
    partner = t + 1 - 2 * lax.rem(t, CORES)
    around = (lax.rem(t + plane, times), lax.rem(t + times - plane, times))
    fore = place_in_line < LINE - 1
    aft = place_in_line > 0
    along = 1 + jnp.logical_and(fore, aft).astype(jnp.int32)
    near_pair = t + CORES * (1 - 2 * lax.rem(place_in_line, 2))
    far_pair = t + 2 * CORES * (1 - 2 * (place_in_line // 2))

    def tell(semaphore, group, strip=s):
        pl.semaphore_signal(semaphore, inc=1, device_id=(group, strip), device_id_type=MESH)

    def tell_around(semaphore):
        for group in around:
            tell(semaphore, group)

        @pl.when(fore)
        def _():
            tell(semaphore, t + CORES)

        @pl.when(aft)
        def _():
            tell(semaphore, t - CORES)

    barrier = pltpu.get_barrier_semaphore()
    @pl.when(jnp.logical_not(jnp.logical_and(follows, upward == 1)))
    def _():
        tell(barrier, t, low)

    @pl.when(jnp.logical_not(jnp.logical_and(follows, upward == 0)))
    def _():
        tell(barrier, t, high)

    tell(barrier, partner)
    tell_around(barrier)

    lanes = [pl.ds(i * LANES, LANES) for i in range(blocks)]
    for k in range(2):
        for i in range(blocks):
            pltpu.make_async_copy(
                c_ref.at[k, :, :, lanes[i]], ext.at[k, :, i, pl.ds(HALO, rows), :], local_sem.at[k]
            ).start()
    opening = [
        pltpu.make_async_copy(c_ref.at[0, :, :, lanes[i]], arrived.at[:, i], local_sem.at[2]) for i in range(blocks)
    ]

    @pl.when(t == 0)
    def _():
        for copy in opening:
            copy.start()

    pl.semaphore_wait(barrier, 5 + along - leads.astype(jnp.int32))

    def halo_copy(side, k, source, target):
        return pltpu.make_async_remote_copy(
            src_ref=source, dst_ref=target, send_sem=halo_send.at[side, k], recv_sem=halo_recv.at[side, k],
            device_id=(t, low if side else high), device_id_type=MESH,
        )

    def halo_start(side, k, source, place):
        for i in range(blocks):
            halo_copy(
                side, k,
                c_ref.at[k, :, pl.ds(source, HALO), lanes[i]],
                ext.at[k, :, i, pl.ds(place, HALO), :],
            ).start()

    def side_start(side, k):
        halo_start(side, k, 0 if side else rows - HALO, HALO + rows if side else 0)

    def far_start():
        relay_start()
        for side in range(2):

            @pl.when(upward == side)
            def _():
                side_start(side, 0)

    def relay_start():
        source = pl.multiple_of((1 - upward) * (rows - HALO), SUBLANES)
        hop = jnp.where(upward == 1, high, low)
        for i in range(blocks):
            pltpu.make_async_remote_copy(
                src_ref=c_ref.at[1, :, pl.ds(source, HALO), lanes[i]], dst_ref=relay.at[:, i],
                send_sem=halo_send.at[upward, 1], recv_sem=relay_recv,
                device_id=(t, hop), device_id_type=MESH,
            ).start()

    @pl.when(follows)
    def _():
        tell(known_in.at[4], t, distant)
        far_start()

    for k in range(2):
        for side in range(2):

            @pl.when(jnp.logical_or(inner, upward != side))
            def _():
                side_start(side, k)

    def relay_copy():
        place = pl.multiple_of(upward * (HALO + rows), SUBLANES)
        return pltpu.make_async_remote_copy(
            src_ref=relay, dst_ref=ext.at[1, :, :, pl.ds(place, HALO), :],
            send_sem=relay_send, recv_sem=halo_recv.at[upward, 1],
            device_id=(t, beyond), device_id_type=MESH,
        )

    tell_around(known_in.at[0])
    pl.semaphore_wait(known_in.at[0], 2 + along)
    for stage_index, group in ((1, near_pair), (2, far_pair), (3, partner)):
        tell(known_in.at[stage_index], group)
        pl.semaphore_wait(known_in.at[stage_index], 1)

    def forward():
        pltpu.make_async_remote_copy(
            src_ref=relay, dst_ref=relay, send_sem=relay_send, recv_sem=relay_recv,
            device_id=(t, high), device_id_type=MESH,
        ).wait_recv()
        relay_copy().start()

    @pl.when(jnp.logical_and(inner, s >= strips // 2))
    def _():
        forward()

    def halo_bytes(side, k):
        part = ext.at[k, :, :, pl.ds(0, HALO), :]
        return pltpu.make_async_remote_copy(
            src_ref=part, dst_ref=part, send_sem=halo_send.at[side, k], recv_sem=halo_recv.at[side, k],
            device_id=(t, high), device_id_type=MESH,
        )

    def propagate(load, count, buffers):
        a = buffers.at[0, :, pl.ds(0, count)]
        b = buffers.at[1, :, pl.ds(0, count)]
        for f in range(3):
            for r in range(count):
                for i in range(blocks):
                    value = load(f, i, r, count)
                    a[f, r, :, i * LANES:(i + 1) * LANES] = value if f == 0 else value * MOMENTUM_SCALE

        def group(_, square):
            for source, target in ((a, b), (b, a)) * (UNROLL // 2):
                step_rows(source, target, square)
                square = square * 0.25
            return square

        lax.fori_loop(0, FACTOR // UNROLL, group, SQUARE_SCALE)
        return lambda f, i, r: a[f, r, :, i * LANES:(i + 1) * LANES] * SCALE_BACK[f]

    center = pl.ds(HALO, half)
    wrapped = t == times - 1

    def back_copy(w):
        return pltpu.make_async_remote_copy(
            src_ref=settled.at[w, 0, :, :, center, :], dst_ref=behind.at[w, :, :, pl.ds(FACTOR, half), :],
            send_sem=back_send.at[w], recv_sem=back_recv.at[w], device_id=(before, s), device_id_type=MESH,
        )

    def on_copy(w, offset):
        return pltpu.make_async_remote_copy(
            src_ref=settled.at[w, 1, :, :, center, :], dst_ref=arrived.at[:, :, pl.ds(offset, half), :],
            send_sem=on_send, recv_sem=on_recv, device_id=(after, s), device_id_type=MESH,
        )

    def send_rows(w, k, offset):
        place = coarse.at[pl.ds(lax.rem(2 * t + 1 + k, 2 * times) * 3, 3)]

        def row_copy(row):
            return pltpu.make_async_remote_copy(
                src_ref=stage.at[w, k, pl.ds((FACTOR + row) * 3, 3)], dst_ref=place,
                send_sem=row_send.at[k], recv_sem=row_recv.at[k],
                device_id=(offset + row, s), device_id_type=MESH,
            )

        @pl.loop(1, half)
        def _(d):
            row_copy(lax.rem(t + d, half)).start()

        last = lax.rem(t, half)

        @pl.when(offset + last != t)
        def _():
            row_copy(last).start()

        @pl.when(offset + last == t)
        def _():
            pltpu.make_async_copy(stage.at[w, k, pl.ds((FACTOR + last) * 3, 3)], place, local_sem.at[3 + k]).start()

    @pl.loop(0, 2)
    def _(w):
        side = lax.rem(w + upward, 2)
        offset = pl.multiple_of(side * half, SUBLANES)

        def advance(k):
            @pl.when(w == 0)
            def _():
                part = ext.at[k, :, :, pl.ds(HALO, rows), :]
                pltpu.make_async_copy(part, part, local_sem.at[k]).wait()

            halo_bytes(side, k).wait_recv()
            result = propagate(
                lambda f, i, r, count: ext[k, f, i, pl.ds(offset + r, SUBLANES, stride=count), :],
                wide // SUBLANES, states,
            )
            for f in range(3):
                for r in range(wide // SUBLANES):
                    for i in range(blocks):
                        settled[side, k, f, i, pl.ds(r, SUBLANES, stride=wide // SUBLANES), :] = result(f, i, r)

        def push(k, buffers):
            return propagate(
                lambda f, i, r, count: settled[side, k, f, i, pl.ds(FACTOR + r, SUBLANES, stride=count), :],
                narrow // SUBLANES, buffers,
            )

        def residual(k, result):
            count = narrow // SUBLANES
            for f in range(3):
                for r in range(count):
                    for i in range(blocks):
                        value = result(f, i, r)
                        if k == 0:
                            known = settled[side, 1, f, i, pl.ds(FACTOR + r, SUBLANES, stride=count), :]
                        else:
                            known = behind[side, f, i, pl.ds(r, SUBLANES, stride=count), :]
                            value = jnp.where(wrapped, known, value)
                        stage[side, k, pl.ds(r * 3 + f, SUBLANES, stride=3 * count), i, :] = value - known

        advance(0)

        @pl.when(jnp.logical_and(w == 0, leads))
        def _():
            pl.semaphore_wait(known_in.at[4], 1)
            far_start()


        back_copy(side).start()
        first = push(0, pushed)
        advance(1)

        residual(0, first)
        send_rows(side, 0, offset)
        @pl.when(jnp.logical_and(w == 0, jnp.logical_and(inner, s < strips // 2)))
        def _():
            forward()

        second = push(1, states)
        back_copy(side).wait_recv()
        residual(1, second)
        send_rows(side, 1, offset)

        @pl.when(jnp.logical_and(t < times - 1, outer))
        def _():
            on_copy(side, offset).start()


    @pl.when(jnp.logical_and(t < times - 1, inner))
    def _():
        for side in range(2):
            on_copy(side, side * half).start()

    for k in range(2):
        for side in range(2):
            halo_bytes(side, k).wait_send()
    for w in range(2):
        back_copy(w).wait_send()

    @pl.when(inner)
    def _():
        relay_copy().wait_send()

    whole = pltpu.make_async_remote_copy(
        src_ref=arrived, dst_ref=arrived, send_sem=on_send, recv_sem=on_recv,
        device_id=(after, s), device_id_type=MESH,
    )

    @pl.when(t == 0)
    def _():
        pltpu.make_async_copy(arrived, arrived, local_sem.at[2]).wait()

    @pl.when(t > 0)
    def _():
        whole.wait_recv()

    @pl.when(t < times - 1)
    def _():
        whole.wait_send()

    for k in range(2):
        part = coarse.at[pl.ds(0, 3 * (times - 1))]
        total = pltpu.make_async_remote_copy(
            src_ref=part, dst_ref=part, send_sem=row_send.at[k], recv_sem=row_recv.at[k],
            device_id=(after, s), device_id_type=MESH,
        )
        total.wait_recv()
        total.wait_send()
        one = coarse.at[pl.ds(0, 3)]
        pltpu.make_async_copy(one, one, local_sem.at[3 + k]).wait()


def place_outputs(arrived, settled, coarse, updated, rows_out, sem):
    half = updated.shape[2] // 2
    for i in range(arrived.shape[1]):
        lane = pl.ds(i * LANES, LANES)
        pltpu.make_async_copy(arrived.at[:, i], updated.at[0, :, :, lane], sem.at[0]).start()
        for side in range(2):
            pltpu.make_async_copy(
                settled.at[side, 0, :, i, pl.ds(HALO, half), :], updated.at[1, :, pl.ds(side * half, half), lane], sem.at[0]
            ).start()
    rows = pltpu.make_async_copy(coarse, rows_out, sem.at[1])
    rows.start()
    pltpu.make_async_copy(updated, updated, sem.at[0]).wait()
    rows.wait()


def solution(mesh):
    def on_device(c_points):
        intervals, fields, rows, columns = c_points.shape
        times = lax.axis_size("tm")
        blocks = columns // LANES
        full = rows + 2 * HALO
        wide = rows // 2 + 2 * HALO
        narrow = rows // 2 + 2 * FACTOR
        f32 = jnp.float32
        arrived, settled, coarse = pl.pallas_call(
            kernel,
            out_shape=(
                pltpu.VMEM((fields, blocks, rows, LANES), f32),
                pltpu.VMEM((2, 2, fields, blocks, wide, LANES), f32),
                pltpu.VMEM((2 * times * fields, blocks, LANES), f32),
            ),
            in_specs=[pl.BlockSpec(memory_space=pl.ANY)],
            out_specs=(pl.BlockSpec(memory_space=pltpu.VMEM),) * 3,
            scratch_shapes=[
                pltpu.VMEM((2, fields, blocks, full, LANES), f32),
                pltpu.VMEM((fields, blocks, HALO, LANES), f32),
                pltpu.VMEM((2, fields, wide // SUBLANES, SUBLANES, columns), f32),
                pltpu.VMEM((2, fields, narrow // SUBLANES, SUBLANES, columns), f32),
                pltpu.VMEM((2, fields, blocks, narrow, LANES), f32),
                pltpu.VMEM((2, 2, narrow * fields, blocks, LANES), f32),
                pltpu.SemaphoreType.DMA((5,)),
                pltpu.SemaphoreType.DMA((2, 2)),
                pltpu.SemaphoreType.DMA((2, 2)),
                pltpu.SemaphoreType.DMA((2,)),
                pltpu.SemaphoreType.DMA((2,)),
                pltpu.SemaphoreType.DMA,
                pltpu.SemaphoreType.DMA,
                pltpu.SemaphoreType.DMA((2,)),
                pltpu.SemaphoreType.DMA((2,)),
                pltpu.SemaphoreType.DMA,
                pltpu.SemaphoreType.DMA,
                pltpu.SemaphoreType.REGULAR((5,)),
            ],
            compiler_params=pltpu.CompilerParams(collective_id=0, has_side_effects=True),
        )(c_points)
        updated, coarse = pl.pallas_call(
            place_outputs,
            out_shape=(jax.ShapeDtypeStruct(c_points.shape, f32), jax.ShapeDtypeStruct(coarse.shape, f32)),
            in_specs=[pl.BlockSpec(memory_space=pl.ANY)] * 3,
            out_specs=(pl.BlockSpec(memory_space=pl.ANY),) * 2,
            scratch_shapes=[pltpu.SemaphoreType.DMA((2,))],
        )(*(pltpu.with_memory_space_constraint(x, pltpu.VMEM) for x in (arrived, settled, coarse)))
        return updated, coarse.reshape(2 * times, fields, 1, 1, columns)

    return jax.shard_map(
        on_device,
        mesh=mesh,
        in_specs=(P("tm", None, "space", None),),
        out_specs=(P("tm", None, "space", None), P(None, None, "space", "tm", None)),
        check_vma=False,
    )
```
